32 devices in a mesh: groups: 2 (over x), seq: 16 (over z, y, core).
Axes of the slice: x: 2, y: 2, z: 4, core: 2. Of those that a mesh axis runs over, the one named last changes fastest.
Arguments:
- mixer_in: bfloat16 [2048, 4608], P(('groups', 'seq')), parts along dimension 0, may hold values from -6 to 6
- gate_in: bfloat16 [2048, 4096], P(('groups', 'seq')), parts along dimension 0, may hold values from -6 to 6
- step_raw: bfloat16 [2048, 64], P(('groups', 'seq')), parts along dimension 0, may hold values from -3 to 3
- step_bias: float32 [64], replicated, may hold values from -1.5 to 0
- rate_log: float32 [64], replicated, as said below
- conv_weight: float32 [4, 4608], replicated, may hold values from -3 to 3
- conv_bias: float32 [4608], replicated, may hold values from -0.5 to 0.5
- skip_gain: float32 [64], replicated, may hold values from 0.5 to 1.5
- norm_gain: float32 [4096], replicated, may hold values from 0.1 to 1.9
- doc_lengths: int32 [12], P('groups'), parts along dimension 0, may hold values from 1 to 512, 1024 in all
Outputs:
- mixed_out: bfloat16 [2048, 4096], P(('groups', 'seq')), parts along dimension 0
The draws below stay inside these ranges and needn't reach their ends.
There are 2 independent parts, one for each index of `groups`. The reference program is written for one: setup_inputs(seed, part) draws one part's arguments, and reference() takes and returns one part's arrays. A program takes and returns all parts, laid end to end along the dimension named above; an argument that names none is the same for every part. Nothing has to cross between parts.
Inputs may be any that keep to these rules, and one draw needn't show every extreme that they name: `doc_lengths`: the 6 lengths of a part sum to 1024, and the longest is exactly 512. exp(rate_log) lies between 0.3 / 1024 and 0.08.
All inputs are finite; a program needn't handle non-finite values.
Results may differ from the reference program's by a relative error of at most 0.0043.
Values may be sent and summed in bfloat16 or wider, within the bound.
No kernel may reach another device: no remote copies, remote signals or barrier semaphores. Data moves between devices by JAX's collectives and lax.ppermute only.
A program may use at most 320 MiB of HBM per device.

```python
import math
import jax
import jax.numpy as jnp
import numpy as np
from jax import lax

HEADS = 64
HEAD_DIM = 64
STATE = 64
GROUPS = 4
CONV = 4
DOCS = 6
TOK_DEV = 64
TOKENS = 1024
INNER = 4096
CH = 4608
DOC_MOST = 512
N_SEQ = 16


def draw_rate_log(key, part):
    chosen_key, levels_key = jax.random.split(jax.random.fold_in(key, 17))
    chosen = jax.random.randint(chosen_key, (HEADS,), 0, 10)
    levels = jax.random.uniform(levels_key, (HEADS,), jnp.float32)
    slow_mark = chosen < 5
    slow_low = math.log(0.3 / TOKENS)
    slow_high = math.log(3.0 / TOKENS)
    fast_low = math.log(0.01)
    fast_high = math.log(0.08)
    slow_part = slow_low + levels * (slow_high - slow_low)
    fast_part = fast_low + levels * (fast_high - fast_low)
    return jnp.where(slow_mark, slow_part, fast_part).astype(jnp.float32)


def steps_of(stream_key, extent, shards, low, high):
    level = 1.0
    for position, blocks in shards:
        heights = jax.random.uniform(jax.random.fold_in(jax.random.fold_in(stream_key, 6), position), (blocks,), jnp.float32, low / len(shards), high / len(shards))
        level = level * jnp.repeat(jnp.exp(heights), extent[position] // blocks).reshape((-1,) + (1,) * (len(extent) - 1 - position))
    return level


def length_profile(amount, total, reach, lean):
    weights = [(1 << 20) // math.isqrt(standing ** lean) + 1 for standing in range(2, amount + 1)]
    rest, given = total - reach - (amount - 1), [1] * (amount - 1)
    while rest > 0:
        movable = [i for i in range(amount - 1) if given[i] < reach]
        whole, remaining = sum([weights[i] for i in movable]), rest
        for i in movable:
            more = min(reach - given[i], max(1, remaining * weights[i] // whole), rest)
            given[i] = given[i] + more
            rest = rest - more
    return np.array([reach] + given)


def uneven_parts(rng, number_of, total, bound, skew):
    if number_of == 2:
        one = jax.random.randint(rng, (), max(1, total - bound), min(bound, total - 1) + 1)
        return jnp.stack([one, total - one])
    tallies = jnp.asarray(length_profile(number_of, total, bound, skew), jnp.int32)
    couples = (number_of - 1) // 2
    donor, sink = tallies[1:1 + 2 * couples:2], tallies[2:2 + 2 * couples:2]
    margin = jnp.minimum(donor - 1, bound - sink)
    shifted = jax.random.randint(jax.random.fold_in(rng, 1), (couples,), 0, 1 << 20) % (margin + 1)
    tallies = tallies.at[1:1 + 2 * couples:2].set(donor - shifted).at[2:2 + 2 * couples:2].set(sink + shifted)
    return tallies[jax.random.permutation(jax.random.fold_in(rng, 2), number_of)]


def noise(own_key, extent, width, bound, shards=(), held_as=jnp.bfloat16):
    gain = steps_of(own_key, extent, shards, -0.22, 0.18) if shards else 1.0
    drawn = jax.random.normal(own_key, extent, jnp.float32) * width * gain
    return jnp.minimum(jnp.maximum(drawn, -bound), bound).astype(held_as)


def setup_inputs(seed: int = 0, part: int = 0) -> dict:
    arg_keys = jax.random.split(jax.random.key(seed), 11)
    part_splits = jax.random.split(jax.random.fold_in(arg_keys[10], part), 11)
    return {
        "mixer_in": noise(part_splits[0], (TOKENS, CH), 1.0, 6.0, ((0, 16),)),
        "gate_in": noise(part_splits[1], (TOKENS, INNER), 1.0, 6.0, ((0, 16),)),
        "step_raw": noise(part_splits[2], (TOKENS, HEADS), 0.5, 3.0, ((0, 16),)),
        "step_bias": jnp.clip(jax.random.uniform(arg_keys[3], (HEADS,), jnp.float32, -1.5, 0.0), -1.5, 0.0),
        "rate_log": draw_rate_log(jax.random.fold_in(arg_keys[10], 71), part),
        "conv_weight": noise(arg_keys[5], (CONV, CH), CONV ** -0.5, 3.0, (), jnp.float32),
        "conv_bias": jnp.clip(jax.random.uniform(arg_keys[6], (CH,), jnp.float32, -0.5, 0.5), -0.5, 0.5),
        "skip_gain": jnp.clip(jax.random.uniform(arg_keys[7], (HEADS,), jnp.float32, 0.5, 1.5), 0.5, 1.5),
        "norm_gain": jnp.clip(1.0 + 0.18 * jax.random.normal(arg_keys[8], (INNER,), jnp.float32), 0.1, 1.9),
        "doc_lengths": uneven_parts(part_splits[9], DOCS, TOKENS, DOC_MOST, 2).astype(jnp.int32),
    }


epsilon = 1e-05

def doc_index(doc_lengths, positions):
    doc_ends = jnp.cumsum(doc_lengths).astype(jnp.int32)
    inside = lax.optimization_barrier(jnp.sum((positions[:, None] >= doc_ends[None, :]).astype(jnp.int32), axis=1))
    return jnp.where(positions >= 0, inside, -1).astype(jnp.int32)

def convolve(tok_block, rim_rows, positions, doc_lengths, conv_weight, conv_bias):
    rim_width = rim_rows.shape[0]
    length = tok_block.shape[0]
    padded = jnp.concatenate([rim_rows, tok_block], axis=0).astype(jnp.float32)
    all_positions = jnp.concatenate([positions[:rim_width] - rim_width, positions]).astype(jnp.int32)
    doc_ids = doc_index(doc_lengths, all_positions)
    own_doc = doc_ids[rim_width:]
    summed = jnp.zeros(tok_block.shape, jnp.float32) + conv_bias[None, :]
    for offset in range(rim_width + 1):
        same_doc = (doc_ids[offset:offset + length] == own_doc)[:, None]
        summed = summed + conv_weight[offset][None, :] * jnp.where(same_doc, padded[offset:offset + length], 0.0)
    return (jax.nn.silu(summed).astype(jnp.bfloat16), own_doc, doc_ids[rim_width - 1])

def group_terms(conv_x, conv_b, conv_c, step_size, log_sums, own_doc, prior_doc, skip_gain, member, group_heads, state_size):
    length = conv_x.shape[0]
    head_size = conv_x.shape[1] // skip_gain.shape[0]
    first = member * group_heads
    picked = slice(first, first + group_heads)
    x_group = conv_x[:, first * head_size:(first + group_heads) * head_size].reshape(length, group_heads, head_size).astype(jnp.float32)
    b_group = conv_b[:, member * state_size:(member + 1) * state_size]
    c_group = conv_c[:, member * state_size:(member + 1) * state_size]
    scores = jnp.dot(c_group, b_group.T, preferred_element_type=jnp.float32)
    places = jnp.arange(length, dtype=jnp.int32)
    causal = (places[:, None] >= places[None, :]) & (own_doc[:, None] == own_doc[None, :])
    head_logs = log_sums[:, picked].T
    log_gaps = head_logs[:, :, None] - head_logs[:, None, :]
    decays = jnp.exp(jnp.where(causal[None], log_gaps, -jnp.inf))
    head_steps = step_size[:, picked].T
    weights = (decays * scores[None] * head_steps[:, None, :]).astype(jnp.bfloat16)
    weights = lax.optimization_barrier(weights).astype(jnp.float32)
    within = jnp.einsum('hts,shp->thp', weights, x_group)
    within = within + skip_gain[picked][None, :, None] * x_group
    final_log = log_sums[-1, picked]
    tail_scale = jnp.exp(final_log[None, :] - log_sums[:, picked]) * step_size[:, picked] * (own_doc == own_doc[-1]).astype(jnp.float32)[:, None]
    weighted = (x_group * tail_scale[:, :, None]).astype(jnp.bfloat16)
    weighted = lax.optimization_barrier(weighted).astype(jnp.float32)
    local_state = jnp.einsum('shp,sn->hpn', weighted, b_group.astype(jnp.float32))
    inward = jnp.exp(log_sums[:, picked]) * (own_doc == prior_doc).astype(jnp.float32)[:, None]
    passing = jnp.exp(final_log) * (own_doc[-1] == prior_doc).astype(jnp.float32)
    return (within, local_state, inward, passing)

def carry_term(c_group, state_in, inward):
    rounded = lax.optimization_barrier(state_in.astype(jnp.bfloat16)).astype(jnp.float32)
    term = jnp.einsum('tn,hpn->thp', c_group.astype(jnp.float32), rounded)
    return term * inward[:, :, None]

def finish(mixed_out, gate_rows, norm_gain):
    length, head_count, head_size = mixed_out.shape
    gated = mixed_out * jax.nn.silu(gate_rows.astype(jnp.float32)).reshape(length, head_count, head_size)
    inv_rms = lax.rsqrt(lax.optimization_barrier(jnp.mean(gated * gated, axis=2, keepdims=True)) + epsilon)
    return ((gated * inv_rms).reshape(length, head_count * head_size) * norm_gain[None, :]).astype(jnp.bfloat16)

def reference(mixer_in, gate_in, step_raw, step_bias, rate_log, conv_weight, conv_bias, skip_gain, norm_gain, doc_lengths):
    rim_width = CONV - 1
    inner_width = HEADS * HEAD_DIM
    group_heads = HEADS // GROUPS

    def advance(carried, block_at):
        state_in, rim_rows = carried
        first_row = (block_at * TOK_DEV).astype(jnp.int32)
        tok_block = lax.dynamic_slice_in_dim(mixer_in, first_row, TOK_DEV, 0)
        gate_rows = lax.dynamic_slice_in_dim(gate_in, first_row, TOK_DEV, 0)
        raw_steps = lax.dynamic_slice_in_dim(step_raw, first_row, TOK_DEV, 0)
        positions = first_row + jnp.arange(TOK_DEV, dtype=jnp.int32)
        mixed, own_doc, prior_doc = convolve(tok_block, rim_rows, positions, doc_lengths, conv_weight, conv_bias)
        mixed = lax.optimization_barrier(mixed)
        conv_x = mixed[:, :inner_width]
        conv_b = mixed[:, inner_width:inner_width + GROUPS * STATE]
        conv_c = mixed[:, inner_width + GROUPS * STATE:]
        step_size = jax.nn.softplus(raw_steps.astype(jnp.float32) + step_bias[None, :])
        log_sums = jnp.cumsum(-jnp.exp(rate_log)[None, :] * step_size, axis=0)
        results = []
        new_states = []
        for member in range(GROUPS):
            within, local_state, inward, passing = group_terms(conv_x, conv_b, conv_c, step_size, log_sums, own_doc, prior_doc, skip_gain, member, group_heads, STATE)
            upper_state = state_in[member * group_heads:(member + 1) * group_heads]
            results.append(within + carry_term(conv_c[:, member * STATE:(member + 1) * STATE], upper_state, inward))
            new_states.append(passing[:, None, None] * upper_state + local_state)
        mixed_out = jnp.concatenate(results, axis=1)
        return ((jnp.concatenate(new_states, axis=0), tok_block[TOK_DEV - rim_width:]), finish(mixed_out, gate_rows, norm_gain))
    initial = (jnp.zeros((HEADS, HEAD_DIM, STATE), jnp.float32), jnp.zeros((rim_width, mixer_in.shape[1]), jnp.bfloat16))
    _, blocks = lax.scan(advance, initial, jnp.arange(N_SEQ, dtype=jnp.int32))
    return blocks.reshape(TOKENS, inner_width)
```

```python
import functools

import jax
import jax.numpy as jnp
from jax import lax
from jax.experimental import pallas as pl
from jax.experimental.pallas import tpu as pltpu
from jax.sharding import PartitionSpec as P

GROUPS = 4
PAIR = 2
RIM = 8
EPSILON = 1e-05
F32 = jnp.float32
BF16 = jnp.bfloat16
VMEM = pl.BlockSpec(memory_space=pltpu.VMEM)
SMEM = pl.BlockSpec(memory_space=pltpu.SMEM)
ANY = pl.BlockSpec(memory_space=pl.ANY)


def dot(a, b, dims=((1,), (0,))):
    return lax.dot_general(a, b, (dims, ((), ())), preferred_element_type=F32)


def silu(v):
    half = 0.5 * v
    return half + half * jnp.tanh(half)


def split(a, parts):
    out = []
    for _ in range(parts):
        top = a.astype(BF16)
        out.append(top)
        a = a - top.astype(F32)
    return out


def doc_of(lengths, position):
    end, found = jnp.int32(0), jnp.zeros_like(position)
    for i in range(lengths.shape[0]):
        end = end + lengths[i]
        found = found + jnp.where(position >= end, 1, 0)
    return jnp.where(position >= 0, found, -1)


def log_sums(raw, bias, rate_log):
    v = raw.astype(F32) + bias
    step = jnp.maximum(v, 0.0) + jnp.log(1.0 + jnp.exp(-jnp.abs(v)))
    change = -jnp.exp(rate_log) * step
    rows = raw.shape[0]
    shape = (rows, 3 * rows)
    behind = lax.broadcasted_iota(jnp.int32, shape, 1) % rows
    lower = jnp.where(behind <= lax.broadcasted_iota(jnp.int32, shape, 0), 1.0, 0.0)
    sums = dot(lower.astype(BF16), jnp.concatenate(split(change, 3), axis=0))
    return step, sums


def selector(heads, columns, width, first):
    shape = (3 * heads, columns)
    head = lax.broadcasted_iota(jnp.int32, shape, 0) % heads
    owner = lax.broadcasted_iota(jnp.int32, shape, 1) // width + first
    return jnp.where(head == owner, 1.0, 0.0).astype(BF16)


def widen(compact, chosen):
    return dot(jnp.concatenate([p.astype(F32) for p in split(compact, 3)], axis=1).astype(BF16), chosen)


def convolve(padded, taps, bias, same):
    width = len(same)
    total = bias + taps[width : width + 1] * padded
    for back in range(1, width + 1):
        moved = pltpu.roll(padded, back, 0)
        total = total + taps[width - back : width - back + 1] * jnp.where(same[back - 1], moved, 0.0)
    return silu(total[RIM:]).astype(BF16)


def same_docs(lengths, first, rows, width):
    position = lax.broadcasted_iota(jnp.int32, (rows + RIM, 128), 0) + (first - RIM)
    doc = doc_of(lengths, position)
    return doc, [pltpu.roll(doc, back, 0) == doc for back in range(1, width + 1)]


def pick(first, a, b):
    return jnp.where(first, a, b)


def states_kernel(keep, dims, lengths, own_hbm, other_hbm, rim_own, rim_other, raw_own, raw_other,
                  step_bias, rate_log, taps, bias, out, out_pass, own, other, own_b, other_b, weighted, sems):
    heads, width, inner, tok = dims
    index = lax.axis_index("seq")
    core, row = index % 2, (index // 2) % 2
    columns = inner // GROUPS
    wanted = row if keep else 1 - row
    group = PAIR * core + wanted
    at = pl.multiple_of(group * columns, columns)
    at_b = pl.multiple_of(inner + core * 128, 128)
    copies = [
        pltpu.make_async_copy(own_hbm.at[:, pl.ds(at, columns)], own, sems.at[0]),
        pltpu.make_async_copy(other_hbm.at[:, pl.ds(at, columns)], other, sems.at[1]),
        pltpu.make_async_copy(own_hbm.at[:, pl.ds(at_b, 128)], own_b, sems.at[2]),
        pltpu.make_async_copy(other_hbm.at[:, pl.ds(at_b, 128)], other_b, sems.at[3]),
    ]
    for copy in copies:
        copy.start()
    is_first = core == 0
    chip_first = (index - core) * tok
    lens = [lengths[i] for i in range(lengths.shape[0])]
    lens = _Lengths(lens)
    doc, same = same_docs(lens, chip_first, 2 * tok, taps.shape[0] - 1)
    prior = doc_of(lens, chip_first - 1)
    end_a = doc_of(lens, chip_first + tok - 1)
    end_b = doc_of(lens, chip_first + 2 * tok - 1)
    raw_a = pick(is_first, raw_own[...].astype(F32), raw_other[...].astype(F32))
    raw_b = pick(is_first, raw_other[...].astype(F32), raw_own[...].astype(F32))
    scales, ends = [], []
    for part, (raw, end) in enumerate(((raw_a, end_a), (raw_b, end_b))):
        step, sums = log_sums(raw, step_bias[...], rate_log[...])
        last = sums[tok - 1 :]
        here = doc[RIM + part * tok : RIM + (part + 1) * tok, :heads] == end
        scales.append(jnp.where(here, jnp.exp(last - sums) * step, 0.0))
        ends.append(jnp.exp(last))
    pass_a = jnp.where(end_a == prior, ends[0], 0.0)
    pass_b = jnp.where(end_b == end_a, ends[1], 0.0)
    rest = jnp.concatenate([pass_b, pass_a * pass_b, jnp.zeros((6, heads), F32)], axis=0)
    scale = widen(jnp.concatenate(scales + [rest], axis=0), selector(heads, columns, width, group * (heads // GROUPS)))
    for copy in copies:
        copy.wait()
    rim_at = pl.ds(at, columns)

    def padded(o, p, rim_columns, lanes):
        a, b = o[:, lanes].astype(F32), p[:, lanes].astype(F32)
        rim = pick(is_first, rim_own[:, rim_columns].astype(F32), rim_other[:, rim_columns].astype(F32))
        return jnp.concatenate([rim, pick(is_first, a, b), pick(is_first, b, a)], axis=0)

    everything = slice(0, 128)
    b_pair = convolve(padded(own_b, other_b, pl.ds(at_b, 128), everything), taps[:, pl.ds(at_b, 128)], bias[:, pl.ds(at_b, 128)], same)
    b_pair = b_pair.astype(F32)
    half = b_pair.shape[1] // 2
    b_rows = pick(wanted == 0, b_pair[:, :half], b_pair[:, half:]).astype(BF16)
    for j in range(columns // 128):
        lanes = slice(j * 128, (j + 1) * 128)
        lanes_at = pl.ds(pl.multiple_of(at + j * 128, 128), 128)
        x = convolve(padded(own, other, lanes_at, lanes), taps[:, lanes_at], bias[:, lanes_at], same)
        weighted[:, lanes] = (x.astype(F32) * scale[: 2 * tok, lanes]).astype(BF16)
    state_a = dot(b_rows[:tok], weighted[:tok], ((0,), (0,)))
    state_b = dot(b_rows[tok:], weighted[tok:], ((0,), (0,)))
    passes = scale[2 * tok + 1 : 2 * tok + 2]
    total = scale[2 * tok : 2 * tok + 1] * state_a + state_b
    out[...] = total.astype(out.dtype)
    if keep:
        out_pass[...] = jnp.broadcast_to(passes, out_pass.shape).astype(out_pass.dtype)
    else:
        out_pass[...] = two_rows(passes, out_pass.shape)


class _Lengths:
    def __init__(self, values):
        self.values, self.shape = values, (len(values),)

    def __getitem__(self, i):
        return self.values[i]


def two_rows(passes, shape):
    top = passes.astype(BF16).astype(F32)
    which = lax.broadcasted_iota(jnp.int32, shape, 0)
    both = jnp.where(which == 0, top, jnp.where(which == 1, passes - top, 0.0))
    return both.astype(BF16)


def one_row(rows):
    wide = rows[...].astype(F32)
    return wide[0:1] + wide[1:2]


def plane_kernel(own, own_pass, got, got_pass, out, out_pass):
    upper = (lax.axis_index("seq") // 2) % 2 == 1
    mine, theirs = own[...], got[...].astype(F32)
    my_pass, their_pass = own_pass[0:1], one_row(got_pass)
    later_pass = pick(upper, my_pass, their_pass)
    total = later_pass * pick(upper, theirs, mine) + pick(upper, mine, theirs)
    out[...] = total.astype(BF16)
    out_pass[...] = two_rows(my_pass * their_pass, out_pass.shape)


def arrive_kernel(reach, own, own_pass, got, got_pass, *rest):
    parts, (out_own, out_sent) = rest[:-2], rest[-2:]
    index = lax.axis_index("seq")
    plane = index // GROUPS
    upper = (index // 2) % 2 == 1
    state = None
    for back in range(reach, 0, -1):
        even, even_pass, odd, odd_pass = parts[4 * (back - 1) : 4 * back]
        source = plane - back
        is_even = (source + 2 * back) // back % 2 == 0
        there = source >= 0
        arrived = pick(is_even, even[...].astype(F32), odd[...].astype(F32))
        arrived = jnp.where(there, arrived, 0.0)
        if state is None:
            state = arrived
        else:
            passes = pick(is_even, one_row(even_pass), one_row(odd_pass))
            state = arrived + jnp.where(there, passes, 0.0) * state
    first_state = pick(upper, got[...].astype(F32), own[...])
    first_pass = pick(upper, one_row(got_pass), own_pass[0:1])
    later = first_pass * state + first_state
    out_own[...] = pick(upper, later, state).astype(BF16)
    out_sent[...] = pick(upper, state, later).astype(BF16)


def local_kernel(dims, lengths, x_ref, bc_ref, before, before_bc, rim, rim_bc, gate, raw, step_bias, rate_log, taps, bias,
                 taps_bc, bias_bc, skip, a_out, b_out, c_out, s_out, p_out, b_all, compact):
    heads, width, state, tok = dims
    g = pl.program_id(0)
    index = lax.axis_index("seq")
    core = index % 2
    is_first = core == 0
    first = index * tok
    lens = _Lengths([lengths[i] for i in range(lengths.shape[0])])
    doc, same = same_docs(lens, first, tok, taps.shape[0] - 1)
    prior = doc_of(lens, first - 1)
    final = doc_of(lens, first + tok - 1)

    def padded(ref, rim_ref, before_ref, lanes):
        top = pick(is_first, rim_ref[:, lanes].astype(F32), before_ref[:, lanes].astype(F32))
        return jnp.concatenate([top, ref[:, lanes].astype(F32)], axis=0)

    @pl.when(g == 0)
    def _():
        for j in range(bc_ref.shape[1] // 128):
            lanes = slice(j * 128, (j + 1) * 128)
            mixed = convolve(padded(bc_ref, rim_bc, before_bc, lanes), taps_bc[:, lanes], bias_bc[:, lanes], same)
            for k in range(128 // state):
                which = j * (128 // state) + k
                value = mixed.astype(F32)[:, k * state : (k + 1) * state].astype(BF16)
                if which < GROUPS:
                    b_all[which] = value
                else:
                    c_out[which - GROUPS] = value
        step, sums = log_sums(raw[...], step_bias[...], rate_log[...])
        last = sums[tok - 1 :]
        rest = jnp.concatenate(
            [jnp.exp(last), jnp.where(final == prior, jnp.exp(last), 0.0), skip[...], jnp.zeros((5, heads), F32)], axis=0)
        whole = jnp.concatenate([jnp.exp(sums), jnp.exp(-sums) * step, rest], axis=0)
        compact[...] = jnp.concatenate([p.astype(F32) for p in split(whole, 3)], axis=1).astype(BF16)

    columns = x_ref.shape[1]
    wide = dot(compact[...], selector(heads, columns, width, g * (heads // GROUPS)))
    inward, outward = wide[:tok], wide[tok : 2 * tok]
    end_decay, passes, gains = (wide[2 * tok + k : 2 * tok + k + 1] for k in range(3))
    b_rows, c_rows = b_all[g], c_out[g]
    scores = dot(c_rows, b_rows, ((1,), (1,)))
    down, across = (lax.broadcasted_iota(jnp.int32, (tok, tok), k) for k in range(2))
    causal = (down >= across) & (doc[RIM:, :tok] == doc_of(lens, across + first))
    mask = jnp.where(causal, scores, 0.0)
    m_top, m_rest = split(mask, 2)
    here = doc[RIM:, :state] == final
    ending = jnp.where(here, b_rows.astype(F32), 0.0).astype(BF16)
    lhs = jnp.concatenate([m_top.astype(F32), m_rest.astype(F32)], axis=1).astype(BF16)
    entered = doc[RIM:] == prior
    for j in range(columns // 128):
        lanes = slice(j * 128, (j + 1) * 128)
        x = convolve(padded(x_ref, rim, before, lanes), taps[:, lanes], bias[:, lanes], same).astype(F32)
        scaled = x * outward[:, lanes]
        s_top, s_rest = split(scaled, 2)
        within = dot(lhs, jnp.concatenate([s_top, s_top], axis=0)) + dot(m_top, s_rest)
        local = dot(ending, s_top, ((0,), (0,))) + dot(ending, s_rest, ((0,), (0,)))
        opened = silu(gate[:, lanes].astype(F32))
        a_out[:, lanes] = (inward[:, lanes] * within + gains[:, lanes] * x) * opened
        b_out[:, lanes] = jnp.where(entered, inward[:, lanes] * opened, 0.0)
        s_out[:, lanes] = (end_decay[:, lanes] * local).astype(BF16)
    p_out[...] = two_rows(passes, p_out.shape)


def finish_kernel(width, a_ref, b_ref, c_ref, prior_state, prior_pass, x0, x1, x2, x3, gain, out):
    index = lax.axis_index("seq")
    core, row = index % 2, (index // 2) % 2
    second = core == 1
    columns = x0.shape[1]
    block = 256
    shape = (2 * block, block)
    r, c = lax.broadcasted_iota(jnp.int32, shape, 0) % block // width, lax.broadcasted_iota(jnp.int32, shape, 1) // width
    means = jnp.where(r == c, 1.0 / width, 0.0).astype(BF16)
    order = ((x0, core, row), (x1, core, 1 - row), (x2, 1 - core, row), (x3, 1 - core, 1 - row))
    for arrived, half, other in order:
        group = PAIR * half + other
        c_rows = c_ref[group]
        for j in range(columns // block):
            lanes = slice(j * block, (j + 1) * block)
            at = pl.ds(pl.multiple_of(group * columns + j * block, block), block)
            state = arrived[:, lanes].astype(F32)
            passes = prior_pass[:, at].astype(F32)
            stepped = (passes[0:1] + passes[1:2]) * state + prior_state[:, at].astype(F32)
            state = pick(second, stepped, state).astype(BF16)
            gated = a_ref[:, at] + b_ref[:, at] * dot(c_rows, state)
            top, rest = split(gated * gated, 2)
            mean = dot(jnp.concatenate([top, rest], axis=1), means)
            out[:, at] = (gated * lax.rsqrt(mean + EPSILON) * gain[:, at]).astype(BF16)


def swap(block, pairs):
    return lax.ppermute(block, "seq", [*pairs, *((b, a) for a, b in pairs)])


def on_device(mixer_in, gate_in, step_raw, step_bias, rate_log, conv_weight, conv_bias, skip_gain, norm_gain, doc_lengths):
    tok, channels = mixer_in.shape
    heads, inner = rate_log.shape[0], gate_in.shape[1]
    width = inner // heads
    state = (channels - inner) // (2 * GROUPS)
    devices = lax.axis_size("seq")
    planes = devices // GROUPS
    columns = inner // GROUPS
    taps_n = conv_weight.shape[0]
    longest = devices * tok // 2
    reach = -(-(longest - 1) // (GROUPS * tok))
    row = lambda a: a.reshape(1, -1)
    step_bias, rate_log, skip_gain, norm_gain, conv_bias = map(row, (step_bias, rate_log, skip_gain, norm_gain, conv_bias))
    cores = [(i, i + 1) for i in range(0, devices, 2)]
    rows = [(i, i + 2) for i in range(0, devices, 4) for i in (i, i + 1)]
    chips = [(i, i + 1) for i in range(1, devices - 1, 2)]

    other = swap(mixer_in, cores)
    other_raw = swap(step_raw, cores)
    rim = swap(mixer_in[tok - RIM :], chips)
    other_rim = swap(rim, cores)

    params = pltpu.CompilerParams(vmem_limit_bytes=48 << 20)

    def states(keep):
        kind = F32 if keep else BF16
        return pl.pallas_call(
            functools.partial(states_kernel, keep, (heads, width, inner, tok)),
            out_shape=(jax.ShapeDtypeStruct((state, columns), kind), jax.ShapeDtypeStruct((8, columns), kind)),
            in_specs=[SMEM, ANY, ANY] + [VMEM] * 8,
            out_specs=(VMEM, VMEM),
            scratch_shapes=[pltpu.VMEM((tok, columns), BF16)] * 2 + [pltpu.VMEM((tok, 128), BF16)] * 2
            + [pltpu.VMEM((2 * tok, columns), BF16), pltpu.SemaphoreType.DMA((4,))],
            compiler_params=params,
            name="states_kept" if keep else "states_sent",
        )(doc_lengths, mixer_in, other, rim, other_rim, step_raw, other_raw, step_bias, rate_log, conv_weight, conv_bias)

    sent, sent_pass = states(False)
    got = swap(sent, rows)
    got_pass = swap(sent_pass, rows)
    kept, kept_pass = states(True)
    piece = jax.ShapeDtypeStruct((state, columns), BF16)
    piece_pass = jax.ShapeDtypeStruct((8, columns), BF16)
    plane, plane_pass = pl.pallas_call(
        plane_kernel, out_shape=(piece, piece_pass), in_specs=[VMEM] * 4, out_specs=(VMEM, VMEM), name="plane_total",
    )(kept, kept_pass, got, got_pass)
    parts = []
    for back in range(1, reach + 1):
        for parity in range(2):
            pairs = [
                (GROUPS * p + q, GROUPS * (p + back) + q)
                for p in range(planes - back) if p // back % 2 == parity
                for q in range(GROUPS)
            ]
            if pairs:
                parts += [swap(plane, pairs), swap(plane_pass, pairs)]
            else:
                parts += parts[-2:]

    def whole(height, length):
        return pl.BlockSpec((height, length), lambda g: (0, 0))

    def by_group(height):
        return pl.BlockSpec((height, columns), lambda g: (0, g))

    rest = channels - inner
    bc = pl.BlockSpec((tok, rest), lambda g: (0, inner // rest))
    last = pl.BlockSpec((RIM, columns), lambda g: (tok // RIM - 1, g))
    last_bc = pl.BlockSpec((RIM, rest), lambda g: (tok // RIM - 1, inner // rest))
    a, b, c, own_state, own_pass = pl.pallas_call(
        functools.partial(local_kernel, (heads, width, state, tok)),
        grid=(GROUPS,),
        out_shape=(
            jax.ShapeDtypeStruct((tok, inner), F32),
            jax.ShapeDtypeStruct((tok, inner), F32),
            jax.ShapeDtypeStruct((GROUPS, tok, state), BF16),
            jax.ShapeDtypeStruct((state, inner), BF16),
            jax.ShapeDtypeStruct((8, inner), BF16),
        ),
        in_specs=[
            SMEM, by_group(tok), bc, last, last_bc, by_group(RIM), pl.BlockSpec((RIM, rest), lambda g: (0, inner // rest)),
            by_group(tok), whole(tok, heads), whole(1, heads), whole(1, heads), by_group(taps_n), by_group(1),
            pl.BlockSpec((taps_n, rest), lambda g: (0, inner // rest)), pl.BlockSpec((1, rest), lambda g: (0, inner // rest)),
            whole(1, heads),
        ],
        out_specs=(by_group(tok), by_group(tok), pl.BlockSpec((GROUPS, tok, state), lambda g: (0, 0, 0)), by_group(state), by_group(8)),
        scratch_shapes=[pltpu.VMEM((GROUPS, tok, state), BF16), pltpu.VMEM((2 * tok + 8, 3 * heads), BF16)],
        compiler_params=params,
        name="local_block",
        cost_estimate=pl.CostEstimate(flops=2 * 10**9, bytes_accessed=8 << 20, transcendentals=10**6),
    )(doc_lengths, mixer_in, mixer_in, other, other, rim, rim, gate_in, step_raw, step_bias, rate_log, conv_weight, conv_bias,
      conv_weight, conv_bias, skip_gain)
    prior_state, prior_pass = swap(own_state, cores), swap(own_pass, cores)

    x0, mine = pl.pallas_call(
        functools.partial(arrive_kernel, reach), out_shape=(piece, piece), in_specs=[VMEM] * (4 + 4 * reach), out_specs=(VMEM, VMEM),
        name="arrive",
    )(kept, kept_pass, got, got_pass, *parts)
    x1 = swap(mine, rows)
    x2 = swap(x0, cores)
    x3 = swap(x1, cores)
    return pl.pallas_call(
        functools.partial(finish_kernel, width),
        out_shape=jax.ShapeDtypeStruct((tok, inner), BF16),
        in_specs=[VMEM] * 10,
        out_specs=VMEM,
        compiler_params=params,
        name="finish",
    )(a, b, c, prior_state, prior_pass, x0, x1, x2, x3, norm_gain)


def solution(mesh):
    split_rows = P(("groups", "seq"), None)
    return jax.shard_map(
        on_device,
        mesh=mesh,
        in_specs=(split_rows, split_rows, split_rows, P(), P(), P(), P(), P(), P(), P("groups")),
        out_specs=split_rows,
        check_vma=False,
    )
```

```python
import functools

import jax
import jax.numpy as jnp
from jax import lax
from jax.experimental import pallas as pl
from jax.experimental.pallas import tpu as pltpu
from jax.sharding import PartitionSpec as P

GROUPS = 4
PAIR = 2
RIM = 8
EPSILON = 1e-05
F32 = jnp.float32
BF16 = jnp.bfloat16
VMEM = pl.BlockSpec(memory_space=pltpu.VMEM)
SMEM = pl.BlockSpec(memory_space=pltpu.SMEM)
ANY = pl.BlockSpec(memory_space=pl.ANY)
HBM = pl.BlockSpec(memory_space=pltpu.HBM)


def dot(a, b, dims=((1,), (0,))):
    return lax.dot_general(a, b, (dims, ((), ())), preferred_element_type=F32)


def silu(v):
    half = 0.5 * v
    return half + half * jnp.tanh(half)


def split(a, parts):
    out = []
    for _ in range(parts):
        top = a.astype(BF16)
        out.append(top)
        a = a - top.astype(F32)
    return out


def doc_of(lengths, position):
    end, found = jnp.int32(0), jnp.zeros_like(position)
    for i in range(lengths.shape[0]):
        end = end + lengths[i]
        found = found + jnp.where(position >= end, 1, 0)
    return jnp.where(position >= 0, found, -1)


def log_sums(raw, bias, rate_log):
    v = raw.astype(F32) + bias
    step = jnp.maximum(v, 0.0) + jnp.log(1.0 + jnp.exp(-jnp.abs(v)))
    change = -jnp.exp(rate_log) * step
    rows = raw.shape[0]
    shape = (rows, 3 * rows)
    behind = lax.broadcasted_iota(jnp.int32, shape, 1) % rows
    lower = jnp.where(behind <= lax.broadcasted_iota(jnp.int32, shape, 0), 1.0, 0.0)
    sums = dot(lower.astype(BF16), jnp.concatenate(split(change, 3), axis=0))
    return step, sums


def selector(heads, columns, width, first):
    shape = (3 * heads, columns)
    head = lax.broadcasted_iota(jnp.int32, shape, 0) % heads
    owner = lax.broadcasted_iota(jnp.int32, shape, 1) // width + first
    return jnp.where(head == owner, 1.0, 0.0).astype(BF16)


def widen(compact, chosen):
    return dot(jnp.concatenate([p.astype(F32) for p in split(compact, 3)], axis=1).astype(BF16), chosen)


def convolve(padded, taps, bias, same):
    width = len(same)
    total = bias + taps[width : width + 1] * padded
    for back in range(1, width + 1):
        moved = pltpu.roll(padded, back, 0)
        total = total + taps[width - back : width - back + 1] * jnp.where(same[back - 1], moved, 0.0)
    return silu(total[RIM:]).astype(BF16)


def same_docs(lengths, first, rows, width):
    position = lax.broadcasted_iota(jnp.int32, (rows + RIM, 128), 0) + (first - RIM)
    doc = doc_of(lengths, position)
    return doc, [pltpu.roll(doc, back, 0) == doc for back in range(1, width + 1)]


def pick(first, a, b):
    return jnp.where(first, a, b)


def prepare_kernel(rows, raw, step_bias, rate_log, rim, tail, inner, sem):
    tok = raw.shape[0]
    copy = pltpu.make_async_copy(rows.at[tok - RIM :], rim, sem)
    copy.start()
    step, sums = log_sums(raw[...], step_bias[...], rate_log[...])
    last = sums[tok - 1 :]
    tail[:tok] = jnp.exp(last - sums) * step
    tail[tok:] = jnp.broadcast_to(jnp.exp(last), (8, raw.shape[1]))
    inner[:tok] = jnp.exp(sums)
    inner[tok:] = jnp.exp(-sums) * step
    copy.wait()


def states_kernel(keep, dims, state, lengths, own_hbm, other, tail_own, tail_other,
                  taps, bias, out, own, own_b, weighted, sems):
    heads, width, inner, tok = dims
    index = lax.axis_index("seq")
    core, row = index % 2, (index // 2) % 2
    columns = inner // GROUPS
    wanted = row if keep else 1 - row
    group = PAIR * core + wanted
    at = pl.multiple_of(group * columns, columns)
    at_b = pl.multiple_of(inner + core * 128, 128)
    copies = [
        pltpu.make_async_copy(own_hbm.at[:, pl.ds(at_b, 128)], own_b, sems.at[0]),
        pltpu.make_async_copy(own_hbm.at[:, pl.ds(at, columns)], own, sems.at[1]),
    ]
    for copy in copies:
        copy.start()
    is_first = core == 0
    chip_first = (index - core) * tok
    lens = [lengths[i] for i in range(lengths.shape[0])]
    lens = _Lengths(lens)
    doc, same = same_docs(lens, chip_first, 2 * tok, taps.shape[0] - 1)
    prior = doc_of(lens, chip_first - 1)
    end_a = doc_of(lens, chip_first + tok - 1)
    end_b = doc_of(lens, chip_first + 2 * tok - 1)
    tail_a = pick(is_first, tail_own[...], tail_other[...])
    tail_b = pick(is_first, tail_other[...], tail_own[...])
    scales, ends = [], []
    for part, (tail, end) in enumerate(((tail_a, end_a), (tail_b, end_b))):
        here = doc[RIM + part * tok : RIM + (part + 1) * tok, :heads] == end
        if part == 0:
            here = here & (lax.broadcasted_iota(jnp.int32, here.shape, 0) >= RIM)
        scales.append(jnp.where(here, tail[:tok], 0.0))
        ends.append(tail[tok : tok + 1])
    pass_a = jnp.where(end_a == prior, ends[0], 0.0)
    pass_b = jnp.where(end_b == end_a, ends[1], 0.0)
    rest = jnp.concatenate([pass_b, pass_a * pass_b, jnp.zeros((6, heads), F32)], axis=0)
    scale = widen(jnp.concatenate(scales + [rest], axis=0), selector(heads, columns, width, group * (heads // GROUPS)))
    for copy in copies:
        copy.wait()

    def padded(o, lanes, lanes_at):
        a, b = o[:, lanes].astype(F32), other[:, lanes_at].astype(F32)
        return jnp.concatenate([jnp.zeros((RIM, a.shape[1]), F32), pick(is_first, a, b), pick(is_first, b, a)], axis=0)

    b_pair = convolve(padded(own_b, slice(0, 128), pl.ds(at_b, 128)), taps[:, pl.ds(at_b, 128)], bias[pl.ds(at_b, 128)].reshape(1, 128), same)
    b_pair = b_pair.astype(F32)
    half = b_pair.shape[1] // 2
    b_rows = pick(wanted == 0, b_pair[:, :half], b_pair[:, half:]).astype(BF16)
    for j in range(columns // 128):
        lanes = slice(j * 128, (j + 1) * 128)
        lanes_at = pl.ds(pl.multiple_of(at + j * 128, 128), 128)
        x = convolve(padded(own, lanes, lanes_at), taps[:, lanes_at], bias[lanes_at].reshape(1, 128), same)
        weighted[:, lanes] = (x.astype(F32) * scale[: 2 * tok, lanes]).astype(BF16)
    state_a = dot(b_rows[:tok], weighted[:tok], ((0,), (0,)))
    state_b = dot(b_rows[tok:], weighted[tok:], ((0,), (0,)))
    passes = scale[2 * tok + 1 : 2 * tok + 2]
    total = scale[2 * tok : 2 * tok + 1] * state_a + state_b
    out[:state] = total.astype(out.dtype)
    if keep:
        out[state:] = jnp.broadcast_to(passes, (8, columns))
    else:
        out[state:] = two_rows(passes, (8, columns))


def rim_kernel(dims, lengths, own_hbm, other, rim_own, rim_other, tail_own, tail_other, taps, bias,
               out_sent, out_kept, own, own_b, sems):
    heads, width, inner, tok = dims
    index = lax.axis_index("seq")
    core, row = index % 2, (index // 2) % 2
    columns = inner // GROUPS
    at = pl.multiple_of(PAIR * core * columns, PAIR * columns)
    at_b = pl.multiple_of(inner + core * 128, 128)
    copies = [
        pltpu.make_async_copy(own_hbm.at[:RIM, pl.ds(at_b, 128)], own_b, sems.at[0]),
        pltpu.make_async_copy(own_hbm.at[:RIM, pl.ds(at, PAIR * columns)], own, sems.at[1]),
    ]
    for copy in copies:
        copy.start()
    is_first = core == 0
    chip_first = (index - core) * tok
    lens = _Lengths([lengths[i] for i in range(lengths.shape[0])])
    doc, same = same_docs(lens, chip_first, RIM, taps.shape[0] - 1)
    end_a = doc_of(lens, chip_first + tok - 1)
    end_b = doc_of(lens, chip_first + 2 * tok - 1)
    here = (doc[RIM:, :heads] == end_a) & (end_b == end_a)
    head_rows = pick(is_first, tail_own[:RIM], tail_other[:RIM])
    end_decay = pick(is_first, tail_other[tok : tok + 1], tail_own[tok : tok + 1])
    scale = jnp.where(here, head_rows * end_decay, 0.0)
    scale = widen(scale, selector(heads, PAIR * columns, width, core * (heads // PAIR)))
    for copy in copies:
        copy.wait()

    def mixed(o, lanes, first):
        lanes_at = pl.ds(pl.multiple_of(first + lanes.start, 128), 128)
        rim = pick(is_first, rim_own[:, lanes_at].astype(F32), rim_other[:, lanes_at].astype(F32))
        rows = jnp.concatenate([rim, pick(is_first, o[:, lanes].astype(F32), other[:RIM, lanes_at].astype(F32))], axis=0)
        return convolve(rows, taps[:, lanes_at], bias[lanes_at].reshape(1, 128), same).astype(F32)

    b_pair = mixed(own_b, slice(0, 128), at_b)
    half = b_pair.shape[1] // 2
    upper = row == 1
    for out, flip in ((out_sent, False), (out_kept, True)):
        which = upper if flip else row == 0
        b_rows = pick(which, b_pair[:, half:], b_pair[:, :half])
        out[RIM:] = jnp.zeros((RIM, columns), BF16)
        out[RIM:, :half] = b_rows.astype(BF16)
    for j in range(columns // 128):
        lanes = slice(j * 128, (j + 1) * 128)
        behind = slice(columns + j * 128, columns + (j + 1) * 128)
        low = mixed(own, lanes, at) * scale[:, lanes]
        high = mixed(own, behind, at) * scale[:, behind]
        out_sent[:RIM, lanes] = pick(upper, low, high).astype(BF16)
        out_kept[:RIM, lanes] = pick(upper, high, low).astype(BF16)


def late(rows):
    half = 64
    return dot(rows[RIM:, :half], rows[:RIM], ((0,), (0,)))


class _Lengths:
    def __init__(self, values):
        self.values, self.shape = values, (len(values),)

    def __getitem__(self, i):
        return self.values[i]


def two_rows(passes, shape):
    top = passes.astype(BF16).astype(F32)
    which = lax.broadcasted_iota(jnp.int32, shape, 0)
    both = jnp.where(which == 0, top, jnp.where(which == 1, passes - top, 0.0))
    return both.astype(BF16)


def one_row(payload):
    wide = payload[-8:].astype(F32)
    return wide[0:1] + wide[1:2]


def plane_kernel(state, own, own_rim, got, got_rim, out, far, base):
    upper = (lax.axis_index("seq") // 2) % 2 == 1
    mine = own[:state] + late(own_rim[...])
    theirs = got[:state].astype(F32) + late(got_rim[...])
    my_pass, their_pass = own[state : state + 1], one_row(got[...])
    first, second = pick(upper, theirs, mine), pick(upper, mine, theirs)
    first_pass, later_pass = pick(upper, their_pass, my_pass), pick(upper, my_pass, their_pass)
    total = (later_pass * first + second).astype(BF16)
    out[:state] = total
    far[...] = total
    out[state:] = two_rows(my_pass * their_pass, (8, own.shape[1]))
    base[:state] = first
    base[state:] = jnp.broadcast_to(first_pass, (8, own.shape[1]))


def arrive_kernel(reach, rows, base, *rest):
    parts, (out_own, out_sent) = rest[:-2], rest[-2:]
    index = lax.axis_index("seq")
    plane = index // GROUPS
    upper = (index // 2) % 2 == 1
    state = None
    for back in range(reach, 0, -1):
        even, odd = parts[2 * (back - 1) : 2 * back]
        source = plane - back
        is_even = (source + 2 * back) // back % 2 == 0
        there = source >= 0
        arrived = jnp.where(there, pick(is_even, even[...].astype(F32), odd[...].astype(F32)), 0.0)
        if state is None:
            state = arrived[:rows]
        else:
            state = arrived[:rows] + one_row(arrived) * state
    later = base[rows : rows + 1] * state + base[:rows]
    out_own[...] = pick(upper, later, state).astype(BF16)
    out_sent[...] = pick(upper, state, later).astype(BF16)


def local_kernel(dims, lengths, x_ref, bc_ref, before, before_bc, rim, rim_bc, gate, tail, decays, taps, bias,
                 taps_bc, bias_bc, skip, a_out, b_out, c_out, s_out, b_all, compact):
    heads, width, state, tok = dims
    g = pl.program_id(0)
    index = lax.axis_index("seq")
    core = index % 2
    is_first = core == 0
    first = index * tok
    lens = _Lengths([lengths[i] for i in range(lengths.shape[0])])
    doc, same = same_docs(lens, first, tok, taps.shape[0] - 1)
    prior = doc_of(lens, first - 1)
    final = doc_of(lens, first + tok - 1)

    def padded(ref, rim_ref, before_ref, lanes):
        top = pick(is_first, rim_ref[:, lanes].astype(F32), before_ref[:, lanes].astype(F32))
        return jnp.concatenate([top, ref[:, lanes].astype(F32)], axis=0)

    @pl.when(g == 0)
    def _():
        for j in range(bc_ref.shape[1] // 128):
            lanes = slice(j * 128, (j + 1) * 128)
            mixed = convolve(padded(bc_ref, rim_bc, before_bc, lanes), taps_bc[:, lanes], bias_bc[:, lanes], same)
            for k in range(128 // state):
                which = j * (128 // state) + k
                value = mixed.astype(F32)[:, k * state : (k + 1) * state].astype(BF16)
                if which < GROUPS:
                    b_all[which] = value
                else:
                    c_out[which - GROUPS] = value
        ending_decay = tail[tok : tok + 1]
        rest = jnp.concatenate(
            [ending_decay, jnp.where(final == prior, ending_decay, 0.0), skip[...], jnp.zeros((5, heads), F32)], axis=0)
        whole = jnp.concatenate([decays[...], rest], axis=0)
        compact[...] = jnp.concatenate([p.astype(F32) for p in split(whole, 3)], axis=1).astype(BF16)

    columns = x_ref.shape[1]
    wide = dot(compact[...], selector(heads, columns, width, g * (heads // GROUPS)))
    inward, outward = wide[:tok], wide[tok : 2 * tok]
    end_decay, passes, gains = (wide[2 * tok + k : 2 * tok + k + 1] for k in range(3))
    b_rows, c_rows = b_all[g], c_out[g]
    scores = dot(c_rows, b_rows, ((1,), (1,)))
    down, across = (lax.broadcasted_iota(jnp.int32, (tok, tok), k) for k in range(2))
    causal = (down >= across) & (doc[RIM:, :tok] == doc_of(lens, across + first))
    mask = jnp.where(causal, scores, 0.0)
    m_top, m_rest = split(mask, 2)
    here = doc[RIM:, :state] == final
    ending = jnp.where(here, b_rows.astype(F32), 0.0).astype(BF16)
    lhs = jnp.concatenate([m_top.astype(F32), m_rest.astype(F32)], axis=1).astype(BF16)
    entered = doc[RIM:] == prior
    for j in range(columns // 128):
        lanes = slice(j * 128, (j + 1) * 128)
        x = convolve(padded(x_ref, rim, before, lanes), taps[:, lanes], bias[:, lanes], same).astype(F32)
        scaled = x * outward[:, lanes]
        s_top, s_rest = split(scaled, 2)
        within = dot(lhs, jnp.concatenate([s_top, s_top], axis=0)) + dot(m_top, s_rest)
        local = dot(ending, s_top, ((0,), (0,))) + dot(ending, s_rest, ((0,), (0,)))
        opened = silu(gate[:, lanes].astype(F32))
        a_out[:, lanes] = (inward[:, lanes] * within + gains[:, lanes] * x) * opened
        b_out[:, lanes] = jnp.where(entered, inward[:, lanes] * opened, 0.0)
        s_out[:state, lanes] = (end_decay[:, lanes] * local).astype(BF16)
    s_out[state:] = two_rows(passes, (8, columns))


def finish_kernel(width, places, a_ref, b_ref, c_ref, prior, gain, *rest):
    arrivals, (out, ready, sems) = rest[: len(places)], rest[-3:]
    index = lax.axis_index("seq")
    core, row = index % 2, (index // 2) % 2
    second = core == 1
    state_rows, columns = arrivals[0].shape
    block = 256
    shape = (2 * block, block)
    r, c = lax.broadcasted_iota(jnp.int32, shape, 0) % block // width, lax.broadcasted_iota(jnp.int32, shape, 1) // width
    means = jnp.where(r == c, 1.0 / width, 0.0).astype(BF16)
    copies = []
    for k, (arrived, (far_core, far_row)) in enumerate(zip(arrivals, places)):
        group = PAIR * (1 - core if far_core else core) + (1 - row if far_row else row)
        c_rows = c_ref[group]
        first = pl.multiple_of(group * columns, columns)
        for j in range(columns // block):
            lanes = slice(j * block, (j + 1) * block)
            at = pl.ds(pl.multiple_of(first + j * block, block), block)
            state = arrived[:, lanes].astype(F32)
            before = prior[:, at].astype(F32)
            stepped = (before[state_rows : state_rows + 1] + before[state_rows + 1 : state_rows + 2]) * state + before[:state_rows]
            state = pick(second, stepped, state).astype(BF16)
            gated = a_ref[:, at] + b_ref[:, at] * dot(c_rows, state)
            top, rest_ = split(gated * gated, 2)
            mean = dot(jnp.concatenate([top, rest_], axis=1), means)
            ready[k, :, lanes] = (gated * lax.rsqrt(mean + EPSILON) * gain[:, at]).astype(BF16)
        copies.append(pltpu.make_async_copy(ready.at[k], out.at[:, pl.ds(first, columns)], sems.at[k]))
        copies[-1].start()
    for copy in copies:
        copy.wait()


def swap(block, pairs):
    return lax.ppermute(block, "seq", [*pairs, *((b, a) for a, b in pairs)])


def on_device(mixer_in, gate_in, step_raw, step_bias, rate_log, conv_weight, conv_bias, skip_gain, norm_gain, doc_lengths):
    tok, channels = mixer_in.shape
    heads, inner = rate_log.shape[0], gate_in.shape[1]
    width = inner // heads
    state = (channels - inner) // (2 * GROUPS)
    devices = lax.axis_size("seq")
    planes = devices // GROUPS
    columns = inner // GROUPS
    taps_n = conv_weight.shape[0]
    longest = devices * tok // 2
    reach = -(-(longest - 1) // (GROUPS * tok))
    row = lambda a: a.reshape(1, -1)
    step_bias, rate_log, skip_gain, norm_gain = map(row, (step_bias, rate_log, skip_gain, norm_gain))
    wide_bias = row(conv_bias)
    cores = [(i, i + 1) for i in range(0, devices, 2)]
    rows = [(i, i + 2) for i in range(0, devices, 4) for i in (i, i + 1)]
    chips = [(i, i + 1) for i in range(1, devices - 1, 2)]

    placed = pltpu.with_memory_space_constraint(mixer_in, pltpu.HBM)
    other = swap(mixer_in, cores)
    rim, tail, decays = pl.pallas_call(
        prepare_kernel,
        out_shape=(jax.ShapeDtypeStruct((RIM, channels), BF16), jax.ShapeDtypeStruct((tok + 8, heads), F32),
                   jax.ShapeDtypeStruct((2 * tok, heads), F32)),
        in_specs=[HBM] + [VMEM] * 3,
        out_specs=(VMEM,) * 3,
        scratch_shapes=[pltpu.SemaphoreType.DMA],
        compiler_params=pltpu.CompilerParams(vmem_limit_bytes=4 << 20),
        name="prepare",
    )(placed, step_raw, step_bias, rate_log)
    other_tail = swap(tail, cores)
    rim = swap(rim, chips)
    other_rim = swap(rim, cores)

    def params(mib):
        return pltpu.CompilerParams(vmem_limit_bytes=mib << 20)

    packed = jax.ShapeDtypeStruct((state + 8, columns), BF16)
    packed_wide = jax.ShapeDtypeStruct((state + 8, columns), F32)
    piece = jax.ShapeDtypeStruct((state, columns), BF16)
    dims = (heads, width, inner, tok)

    def states(keep):
        return pl.pallas_call(
            functools.partial(states_kernel, keep, dims, state),
            out_shape=packed_wide if keep else packed,
            in_specs=[SMEM, HBM] + [VMEM] * 5,
            out_specs=VMEM,
            scratch_shapes=[pltpu.VMEM((tok, columns), BF16), pltpu.VMEM((tok, 128), BF16),
                            pltpu.VMEM((2 * tok, columns), BF16), pltpu.SemaphoreType.DMA((2,))],
            compiler_params=params(8),
            name="states_kept" if keep else "states_sent",
        )(doc_lengths, placed, other, tail, other_tail, conv_weight, conv_bias)

    sent = states(False)
    got = swap(sent, rows)
    kept = states(True)
    corner = jax.ShapeDtypeStruct((2 * RIM, columns), BF16)
    rim_sent, rim_kept = pl.pallas_call(
        functools.partial(rim_kernel, dims),
        out_shape=(corner, corner),
        in_specs=[SMEM, HBM] + [VMEM] * 7,
        out_specs=(VMEM, VMEM),
        scratch_shapes=[pltpu.VMEM((RIM, PAIR * columns), BF16), pltpu.VMEM((RIM, 128), BF16), pltpu.SemaphoreType.DMA((2,))],
        compiler_params=params(4),
        name="rim_terms",
    )(doc_lengths, placed, other, rim, other_rim, tail, other_tail, conv_weight, conv_bias)
    rim_got = swap(rim_sent, rows)
    plane, far, base = pl.pallas_call(
        functools.partial(plane_kernel, state), out_shape=(packed, piece, packed_wide), in_specs=[VMEM] * 4, out_specs=(VMEM,) * 3,
        compiler_params=params(4), name="plane_total",
    )(kept, rim_kept, got, rim_got)
    parts = []
    for back in range(1, reach + 1):
        for parity in range(2):
            pairs = [
                (GROUPS * p + q, GROUPS * (p + back) + q)
                for p in range(planes - back) if p // back % 2 == parity
                for q in range(GROUPS)
            ]
            payload = far if back == reach else plane
            parts.append(swap(payload, pairs) if pairs else parts[-1])

    def whole(height, length):
        return pl.BlockSpec((height, length), lambda g: (0, 0))

    def by_group(height):
        return pl.BlockSpec((height, columns), lambda g: (0, g))

    rest = channels - inner
    bc = pl.BlockSpec((tok, rest), lambda g: (0, inner // rest))
    last = pl.BlockSpec((RIM, columns), lambda g: (tok // RIM - 1, g))
    last_bc = pl.BlockSpec((RIM, rest), lambda g: (tok // RIM - 1, inner // rest))
    a, b, c, own_state = pl.pallas_call(
        functools.partial(local_kernel, (heads, width, state, tok)),
        grid=(GROUPS,),
        out_shape=(
            jax.ShapeDtypeStruct((tok, inner), F32),
            jax.ShapeDtypeStruct((tok, inner), F32),
            jax.ShapeDtypeStruct((GROUPS, tok, state), BF16),
            jax.ShapeDtypeStruct((state + 8, inner), BF16),
        ),
        in_specs=[
            SMEM, by_group(tok), bc, last, last_bc, by_group(RIM), pl.BlockSpec((RIM, rest), lambda g: (0, inner // rest)),
            by_group(tok), whole(tok + 8, heads), whole(2 * tok, heads), by_group(taps_n), by_group(1),
            pl.BlockSpec((taps_n, rest), lambda g: (0, inner // rest)), pl.BlockSpec((1, rest), lambda g: (0, inner // rest)),
            whole(1, heads),
        ],
        out_specs=(by_group(tok), by_group(tok), pl.BlockSpec((GROUPS, tok, state), lambda g: (0, 0, 0)), by_group(state + 8)),
        scratch_shapes=[pltpu.VMEM((GROUPS, tok, state), BF16), pltpu.VMEM((2 * tok + 8, 3 * heads), BF16)],
        compiler_params=params(16),
        name="local_block",
        cost_estimate=pl.CostEstimate(flops=2 * 10**9, bytes_accessed=8 << 20, transcendentals=10**6),
    )(doc_lengths, mixer_in, mixer_in, other, other, rim, rim, gate_in, tail, decays, conv_weight, wide_bias,
      conv_weight, wide_bias, skip_gain)
    prior = swap(own_state, cores)

    x0, mine = pl.pallas_call(
        functools.partial(arrive_kernel, reach, state), out_shape=(piece, piece), in_specs=[VMEM] * (1 + 2 * reach),
        out_specs=(VMEM, VMEM), compiler_params=params(4), name="arrive",
    )(base, *parts)
    x1 = swap(mine, rows)
    x2 = swap(x0, cores)
    x3 = swap(x1, cores)

    def finish(out, places, *arrivals):
        count = len(places)
        return pl.pallas_call(
            functools.partial(finish_kernel, width, places),
            out_shape=jax.ShapeDtypeStruct((tok, inner), BF16),
            in_specs=[VMEM] * (5 + count) + [HBM] * (out is not None),
            out_specs=HBM,
            scratch_shapes=[pltpu.VMEM((count, tok, columns), BF16), pltpu.SemaphoreType.DMA((count,))],
            input_output_aliases={} if out is None else {5 + count: 0},
            compiler_params=params(8),
        )(a, b, c, prior, norm_gain, *arrivals, *([] if out is None else [out]))

    out = finish(None, ((False, False), (True, False)), x0, x2)
    out = finish(out, ((False, True),), x1)
    return finish(out, ((True, True),), x3)


def solution(mesh):
    split_rows = P(("groups", "seq"), None)
    return jax.shard_map(
        on_device,
        mesh=mesh,
        in_specs=(split_rows, split_rows, split_rows, P(), P(), P(), P(), P(), P(), P("groups")),
        out_specs=split_rows,
        check_vma=False,
    )
```

```python
import functools

import jax
import jax.numpy as jnp
from jax import lax
from jax.experimental import pallas as pl
from jax.experimental.pallas import tpu as pltpu
from jax.sharding import PartitionSpec as P

GROUPS = 4
PAIR = 2
RIM = 8
EPSILON = 1e-05
F32 = jnp.float32
BF16 = jnp.bfloat16
VMEM = pl.BlockSpec(memory_space=pltpu.VMEM)
HBM = pl.BlockSpec(memory_space=pltpu.HBM)


def dot(a, b, dims=((1,), (0,))):
    return lax.dot_general(a, b, (dims, ((), ())), preferred_element_type=F32)


def silu(v):
    half = 0.5 * v
    return half + half * jnp.tanh(half)


def split(a, parts):
    out = []
    for _ in range(parts):
        top = a.astype(BF16)
        out.append(top)
        a = a - top.astype(F32)
    return out


def doc_of(ends, position):
    found = jnp.zeros(position.shape, jnp.int32)
    for i in range(ends.shape[0]):
        found = found + jnp.where(position >= ends[i : i + 1, : position.shape[1]], 1, 0)
    return jnp.where(position >= 0, found, -1)


def doc_at(ends, place):
    return doc_of(ends, jnp.broadcast_to(place, (1, ends.shape[1])))


def log_sums(raw, bias, rate_log):
    v = raw.astype(F32) + bias
    step = jnp.maximum(v, 0.0) + jnp.log(1.0 + jnp.exp(-jnp.abs(v)))
    change = -jnp.exp(rate_log) * step
    down, across = (lax.broadcasted_iota(jnp.int32, (raw.shape[0],) * 2, k) for k in range(2))
    lower = jnp.where(across <= down, 1.0, 0.0).astype(BF16)
    sums = sum(dot(lower, part) for part in split(change, 3))
    return step, sums


def selector(heads, columns, width, first):
    start = (lax.broadcasted_iota(jnp.int32, (heads, 128), 0) - first) * width
    lane = lax.broadcasted_iota(jnp.int32, (heads, 128), 1)
    tiles = []
    for j in range(columns // 128):
        column = lane + j * 128
        tiles.append(jnp.where((column >= start) & (column < start + width), 1.0, 0.0))
    once = jnp.concatenate(tiles, axis=1).astype(BF16)
    return jnp.concatenate([once] * 3, axis=0)


def widen(compact, chosen):
    return dot(jnp.concatenate([p.astype(F32) for p in split(compact, 3)], axis=1).astype(BF16), chosen)


def convolve(padded, taps, bias, same):
    width = len(same)
    total = bias + taps[width : width + 1] * padded
    for back in range(1, width + 1):
        moved = pltpu.roll(padded, back, 0)
        total = total + taps[width - back : width - back + 1] * jnp.where(same[back - 1], moved, 0.0)
    return silu(total[RIM:]).astype(BF16)


def same_docs(ends, first, rows, width):
    position = lax.broadcasted_iota(jnp.int32, (rows + RIM, 128), 0) + (first - RIM)
    doc = doc_of(ends, position)
    return doc, [pltpu.roll(doc, back, 0) == doc for back in range(1, width + 1)]


def pick(first, a, b):
    return jnp.where(first, a, b)


def load_kernel(lengths, rows, raw, step_bias, rate_log, taps, bias, out_rows, rim, out_raw, out_bias, out_rate, out_taps,
                out_conv, ends, lens, sems):
    tok = rows.shape[0]
    moves = [
        (lengths, lens), (rows.at[tok - RIM :], rim), (raw, out_raw), (step_bias, out_bias), (rate_log, out_rate),
        (taps, out_taps), (bias, out_conv), (rows, out_rows),
    ]
    copies = [pltpu.make_async_copy(a, b, sems.at[k]) for k, (a, b) in enumerate(moves)]
    for copy in copies:
        copy.start()
    copies[0].wait()
    end = jnp.int32(0)
    for i in range(lengths.shape[0]):
        end = end + lens[i]
        ends[i : i + 1] = jnp.broadcast_to(end, (1, 128))
    for copy in copies[1:]:
        copy.wait()


def states_kernel(keep, dims, state, ends_ref, own, other, *rest):
    heads, width, inner, tok = dims
    if keep:
        compact, taps, bias, out, weighted = rest
    else:
        raw_own, raw_other, step_bias, rate_log, taps, bias, out, compact, weighted = rest
    index = lax.axis_index("seq")
    core, row = index % 2, (index // 2) % 2
    columns = inner // GROUPS
    wanted = row if keep else 1 - row
    group = PAIR * core + wanted
    at = pl.multiple_of(group * columns, columns)
    at_b = pl.multiple_of(inner + core * 128, 128)
    is_first = core == 0
    chip_first = (index - core) * tok
    ends = ends_ref[...]
    doc, same = same_docs(ends, chip_first, 2 * tok, taps.shape[0] - 1)
    if not keep:
        prior, end_a, end_b = (
            doc_at(ends, chip_first + place)[:, :heads] for place in (-1, tok - 1, 2 * tok - 1)
        )
        one, two = (log_sums(raw[...], step_bias[...], rate_log[...]) for raw in (raw_own, raw_other))
        scales, lasts = [], []
        for part, end in enumerate((end_a, end_b)):
            step, sums = (pick(is_first == (part == 0), a, b) for a, b in zip(one, two))
            last = sums[tok - 1 :]
            here = doc[RIM + part * tok : RIM + (part + 1) * tok, :heads] == end
            scales.append(jnp.where(here, jnp.exp(last - sums) * step, 0.0))
            lasts.append(jnp.exp(last))
        pass_a = jnp.where(end_a == prior, lasts[0], 0.0)
        pass_b = jnp.where(end_b == end_a, lasts[1], 0.0)
        compact[:RIM] = jnp.zeros((RIM, heads), F32)
        compact[RIM:tok] = scales[0][RIM:]
        compact[tok : 2 * tok] = scales[1]
        which = lax.broadcasted_iota(jnp.int32, (8, heads), 0)
        compact[2 * tok : 2 * tok + 8] = jnp.where(which == 0, pass_b, jnp.where(which == 1, pass_a * pass_b, 0.0))
        compact[2 * tok + 8 :] = scales[0][:RIM] * pass_b
    scale = widen(compact[: 2 * tok + 8], selector(heads, columns, width, group * (heads // GROUPS)))

    def padded(lanes_at):
        a, b = own[:, lanes_at].astype(F32), other[:, lanes_at].astype(F32)
        return jnp.concatenate([jnp.zeros((RIM, a.shape[1]), F32), pick(is_first, a, b), pick(is_first, b, a)], axis=0)

    here_b = pl.ds(at_b, 128)
    b_pair = convolve(padded(here_b), taps[:, here_b], bias[here_b].reshape(1, 128), same).astype(F32)
    half = b_pair.shape[1] // 2
    b_rows = pick(wanted == 0, b_pair[:, :half], b_pair[:, half:]).astype(BF16)
    for j in range(columns // 128):
        lanes = slice(j * 128, (j + 1) * 128)
        lanes_at = pl.ds(pl.multiple_of(at + j * 128, 128), 128)
        x = convolve(padded(lanes_at), taps[:, lanes_at], bias[lanes_at].reshape(1, 128), same)
        weighted[:, lanes] = (x.astype(F32) * scale[: 2 * tok, lanes]).astype(BF16)
    state_a = dot(b_rows[:tok], weighted[:tok], ((0,), (0,)))
    state_b = dot(b_rows[tok:], weighted[tok:], ((0,), (0,)))
    passes = scale[2 * tok + 1 : 2 * tok + 2]
    total = scale[2 * tok : 2 * tok + 1] * state_a + state_b
    out[:state] = total.astype(out.dtype)
    if keep:
        out[state:] = jnp.broadcast_to(passes, (8, columns))
    else:
        out[state:] = two_rows(passes, (8, columns))


def rim_kernel(dims, ends, own, other, rim_own, rim_other, compact, taps, bias, out_sent, out_kept):
    heads, width, inner, tok = dims
    index = lax.axis_index("seq")
    core, row = index % 2, (index // 2) % 2
    columns = inner // GROUPS
    at = pl.multiple_of(PAIR * core * columns, PAIR * columns)
    at_b = pl.multiple_of(inner + core * 128, 128)
    is_first = core == 0
    chip_first = (index - core) * tok
    _, same = same_docs(ends[...], chip_first, RIM, taps.shape[0] - 1)
    scale = widen(compact[2 * tok + 8 :], selector(heads, PAIR * columns, width, core * (heads // PAIR)))

    def mixed(lanes_at):
        rim = pick(is_first, rim_own[:, lanes_at].astype(F32), rim_other[:, lanes_at].astype(F32))
        top = pick(is_first, own[:RIM, lanes_at].astype(F32), other[:RIM, lanes_at].astype(F32))
        rows = jnp.concatenate([rim, top], axis=0)
        return convolve(rows, taps[:, lanes_at], bias[lanes_at].reshape(1, 128), same).astype(F32)

    b_pair = mixed(pl.ds(at_b, 128))
    half = b_pair.shape[1] // 2
    upper = row == 1
    for out, which in ((out_sent, row == 0), (out_kept, upper)):
        b_rows = pick(which, b_pair[:, half:], b_pair[:, :half])
        out[RIM:] = jnp.zeros((RIM, columns), BF16)
        out[RIM:, :half] = b_rows.astype(BF16)
    for j in range(columns // 128):
        lanes = slice(j * 128, (j + 1) * 128)
        behind = slice(columns + j * 128, columns + (j + 1) * 128)
        low = mixed(pl.ds(pl.multiple_of(at + j * 128, 128), 128)) * scale[:, lanes]
        high = mixed(pl.ds(pl.multiple_of(at + columns + j * 128, 128), 128)) * scale[:, behind]
        out_sent[:RIM, lanes] = pick(upper, low, high).astype(BF16)
        out_kept[:RIM, lanes] = pick(upper, high, low).astype(BF16)


def late(rows, state):
    return dot(rows[RIM:, :state], rows[:RIM], ((0,), (0,)))


def two_rows(passes, shape):
    top = passes.astype(BF16).astype(F32)
    which = lax.broadcasted_iota(jnp.int32, shape, 0)
    both = jnp.where(which == 0, top, jnp.where(which == 1, passes - top, 0.0))
    return both.astype(BF16)


def one_row(payload):
    wide = payload[-8:].astype(F32)
    return wide[0:1] + wide[1:2]


def plane_kernel(state, own, own_rim, got, got_rim, out, far, base):
    upper = (lax.axis_index("seq") // 2) % 2 == 1
    mine = own[:state] + late(own_rim[...], state)
    theirs = got[:state].astype(F32) + late(got_rim[...], state)
    my_pass, their_pass = own[state : state + 1], one_row(got[...])
    first, second = pick(upper, theirs, mine), pick(upper, mine, theirs)
    first_pass, later_pass = pick(upper, their_pass, my_pass), pick(upper, my_pass, their_pass)
    total = (later_pass * first + second).astype(BF16)
    out[:state] = total
    far[...] = total
    out[state:] = two_rows(my_pass * their_pass, (8, own.shape[1]))
    base[:state] = first
    base[state:] = jnp.broadcast_to(first_pass, (8, own.shape[1]))


def arrive_kernel(reach, rows, base, *rest):
    parts, (out_own, out_sent) = rest[:-2], rest[-2:]
    index = lax.axis_index("seq")
    plane = index // GROUPS
    upper = (index // 2) % 2 == 1
    state = None
    for back in range(reach, 0, -1):
        even, odd = parts[2 * (back - 1) : 2 * back]
        source = plane - back
        is_even = (source + 2 * back) // back % 2 == 0
        there = source >= 0
        arrived = jnp.where(there, pick(is_even, even[...].astype(F32), odd[...].astype(F32)), 0.0)
        if state is None:
            state = arrived[:rows]
        else:
            state = arrived[:rows] + one_row(arrived) * state
    later = base[rows : rows + 1] * state + base[:rows]
    out_own[...] = pick(upper, later, state).astype(BF16)
    out_sent[...] = pick(upper, state, later).astype(BF16)


def local_kernel(dims, ends_ref, x_ref, bc_ref, before, before_bc, rim, rim_bc, gate, raw, step_bias, rate_log, taps, bias,
                 taps_bc, bias_bc, skip, a_out, b_out, c_out, s_out, b_all, compact):
    heads, width, state, tok = dims
    g = pl.program_id(0)
    index = lax.axis_index("seq")
    core = index % 2
    is_first = core == 0
    first = index * tok
    ends = ends_ref[...]
    doc, same = same_docs(ends, first, tok, taps.shape[0] - 1)
    prior = doc_at(ends, first - 1)
    final = doc_at(ends, first + tok - 1)

    def padded(ref, rim_ref, before_ref, lanes):
        top = pick(is_first, rim_ref[:, lanes].astype(F32), before_ref[:, lanes].astype(F32))
        return jnp.concatenate([top, ref[:, lanes].astype(F32)], axis=0)

    @pl.when(g == 0)
    def _():
        for j in range(bc_ref.shape[1] // 128):
            lanes = slice(j * 128, (j + 1) * 128)
            mixed = convolve(padded(bc_ref, rim_bc, before_bc, lanes), taps_bc[:, lanes], bias_bc[:, lanes], same)
            for k in range(128 // state):
                which = j * (128 // state) + k
                value = mixed.astype(F32)[:, k * state : (k + 1) * state].astype(BF16)
                if which < GROUPS:
                    b_all[which] = value
                else:
                    c_out[which - GROUPS] = value
        step, sums = log_sums(raw[...], step_bias[...], rate_log[...])
        ending_decay = jnp.exp(sums[tok - 1 :])
        passed = jnp.where((final == prior)[:, :heads], ending_decay, 0.0)
        rest = jnp.concatenate([ending_decay, passed, skip[...], jnp.zeros((5, heads), F32)], axis=0)
        whole = jnp.concatenate([jnp.exp(sums), jnp.exp(-sums) * step, rest], axis=0)
        compact[...] = jnp.concatenate([p.astype(F32) for p in split(whole, 3)], axis=1).astype(BF16)

    columns = x_ref.shape[1]
    wide = dot(compact[...], selector(heads, columns, width, g * (heads // GROUPS)))
    inward, outward = wide[:tok], wide[tok : 2 * tok]
    end_decay, passes, gains = (wide[2 * tok + k : 2 * tok + k + 1] for k in range(3))
    b_rows, c_rows = b_all[g], c_out[g]
    scores = dot(c_rows, b_rows, ((1,), (1,)))
    down, across = (lax.broadcasted_iota(jnp.int32, (tok, tok), k) for k in range(2))
    causal = (down >= across) & (doc[RIM:, :tok] == doc_of(ends, across + first))
    mask = jnp.where(causal, scores, 0.0)
    m_top, m_rest = split(mask, 2)
    here = doc[RIM:, :state] == final[:, :state]
    ending = jnp.where(here, b_rows.astype(F32), 0.0).astype(BF16)
    lhs = jnp.concatenate([m_top.astype(F32), m_rest.astype(F32)], axis=1).astype(BF16)
    entered = doc[RIM:] == prior
    for j in range(columns // 128):
        lanes = slice(j * 128, (j + 1) * 128)
        x = convolve(padded(x_ref, rim, before, lanes), taps[:, lanes], bias[:, lanes], same).astype(F32)
        scaled = x * outward[:, lanes]
        s_top, s_rest = split(scaled, 2)
        within = dot(lhs, jnp.concatenate([s_top, s_top], axis=0)) + dot(m_top, s_rest)
        local = dot(ending, s_top, ((0,), (0,))) + dot(ending, s_rest, ((0,), (0,)))
        opened = silu(gate[:, lanes].astype(F32))
        a_out[:, lanes] = (inward[:, lanes] * within + gains[:, lanes] * x) * opened
        b_out[:, lanes] = jnp.where(entered, inward[:, lanes] * opened, 0.0)
        s_out[:state, lanes] = (end_decay[:, lanes] * local).astype(BF16)
    s_out[state:] = two_rows(passes, (8, columns))


def place_of(far_core, far_row):
    index = lax.axis_index("seq")
    core, row = index % 2, (index // 2) % 2
    return PAIR * (1 - core if far_core else core) + (1 - row if far_row else row)


def finish_piece(width, group, arrived, a_ref, b_ref, c_ref, prior, gain, put):
    second = lax.axis_index("seq") % 2 == 1
    state_rows, columns = arrived.shape
    block = 256
    down, across = (lax.broadcasted_iota(jnp.int32, (block, block), k) for k in range(2))
    low = across - lax.rem(across, width)
    means = jnp.where((down >= low) & (down < low + width), 1.0 / width, 0.0).astype(BF16)
    c_rows = c_ref[group]
    for j in range(columns // block):
        lanes = slice(j * block, (j + 1) * block)
        at = pl.ds(pl.multiple_of(group * columns + j * block, block), block)
        state = arrived[:, lanes].astype(F32)
        before = prior[:, at].astype(F32)
        stepped = (before[state_rows : state_rows + 1] + before[state_rows + 1 : state_rows + 2]) * state + before[:state_rows]
        state = pick(second, stepped, state).astype(BF16)
        gated = a_ref[:, at] + b_ref[:, at] * dot(c_rows, state)
        top, rest = split(gated * gated, 2)
        mean = dot(top, means) + dot(rest, means)
        put(lanes, (gated * lax.rsqrt(mean + EPSILON) * gain[:, at]).astype(BF16))


def finish_near_kernel(width, a, b, c, prior, gain, x0, x2, out, ready, sems):
    columns, copies = x0.shape[1], []
    for k, arrived in enumerate((x0, x2)):
        group = place_of(k == 1, False)

        def put(lanes, value, k=k):
            ready[k, :, lanes] = value

        finish_piece(width, group, arrived, a, b, c, prior, gain, put)
        target = out.at[:, pl.ds(pl.multiple_of(group * columns, columns), columns)]
        copies.append(pltpu.make_async_copy(ready.at[k], target, sems.at[k]))
        copies[-1].start()
    for copy in copies:
        copy.wait()


def finish_back_kernel(width, a, b, c, prior, gain, x1, out):
    def put(lanes, value):
        out[:, lanes] = value

    finish_piece(width, place_of(False, True), x1, a, b, c, prior, gain, put)


def finish_far_kernel(width, a, b, c, prior, gain, x3, piece, begun, out, ready, sems):
    columns = x3.shape[1]

    def target(group):
        return out.at[:, pl.ds(pl.multiple_of(group * columns, columns), columns)]

    early = pltpu.make_async_copy(piece, target(place_of(False, True)), sems.at[0])
    early.start()

    def put(lanes, value):
        ready[:, lanes] = value

    group = place_of(True, True)
    finish_piece(width, group, x3, a, b, c, prior, gain, put)
    copy = pltpu.make_async_copy(ready, target(group), sems.at[1])
    copy.start()
    early.wait()
    copy.wait()


def swap(block, pairs):
    return lax.ppermute(block, "seq", [*pairs, *((b, a) for a, b in pairs)])


def on_device(mixer_in, gate_in, step_raw, step_bias, rate_log, conv_weight, conv_bias, skip_gain, norm_gain, doc_lengths):
    tok, channels = mixer_in.shape
    heads, inner = rate_log.shape[0], gate_in.shape[1]
    width = inner // heads
    state = (channels - inner) // (2 * GROUPS)
    devices = lax.axis_size("seq")
    planes = devices // GROUPS
    columns = inner // GROUPS
    taps_n = conv_weight.shape[0]
    longest = devices * tok // 2
    reach = -(-(longest - 1) // (GROUPS * tok))
    row = lambda a: a.reshape(1, -1)
    step_bias, rate_log, skip_gain, norm_gain, wide_bias = map(row, (step_bias, rate_log, skip_gain, norm_gain, conv_bias))
    cores = [(i, i + 1) for i in range(0, devices, 2)]
    rows = [(i, i + 2) for i in range(0, devices, 4) for i in (i, i + 1)]
    chips = [(i, i + 1) for i in range(1, devices - 1, 2)]

    def hbm(block):
        return pltpu.with_memory_space_constraint(block, pltpu.HBM)

    other = swap(mixer_in, cores)
    other_raw = swap(step_raw, cores)
    own, rim, raw, step_bias, rate_log, taps, bias, ends = pl.pallas_call(
        load_kernel,
        out_shape=(
            jax.ShapeDtypeStruct((tok, channels), BF16), jax.ShapeDtypeStruct((RIM, channels), BF16),
            jax.ShapeDtypeStruct((tok, heads), BF16), jax.ShapeDtypeStruct((1, heads), F32),
            jax.ShapeDtypeStruct((1, heads), F32), jax.ShapeDtypeStruct((taps_n, channels), F32),
            jax.ShapeDtypeStruct((channels,), F32), jax.ShapeDtypeStruct((doc_lengths.shape[0], 128), jnp.int32),
        ),
        in_specs=[HBM] * 7,
        out_specs=(VMEM,) * 8,
        scratch_shapes=[pltpu.SMEM(doc_lengths.shape, jnp.int32), pltpu.SemaphoreType.DMA((8,))],
        compiler_params=pltpu.CompilerParams(vmem_limit_bytes=4 << 20),
        name="load",
    )(*map(hbm, (doc_lengths, mixer_in, step_raw, step_bias, rate_log, conv_weight, conv_bias)))
    rim = swap(rim, chips)
    other_rim = swap(rim, cores)

    def params(mib):
        return pltpu.CompilerParams(vmem_limit_bytes=mib << 20)

    packed = jax.ShapeDtypeStruct((state + 8, columns), BF16)
    packed_wide = jax.ShapeDtypeStruct((state + 8, columns), F32)
    piece = jax.ShapeDtypeStruct((state, columns), BF16)
    dims = (heads, width, inner, tok)

    def states(keep, *operands):
        compact = () if keep else (jax.ShapeDtypeStruct((2 * tok + 16, heads), F32),)
        return pl.pallas_call(
            functools.partial(states_kernel, keep, dims, state),
            out_shape=(packed_wide if keep else packed, *compact),
            in_specs=[VMEM] * (3 + len(operands) + 2),
            out_specs=(VMEM,) * (1 + len(compact)),
            scratch_shapes=[pltpu.VMEM((2 * tok, columns), BF16)],
            compiler_params=params(8),
            name="states_kept" if keep else "states_sent",
        )(ends, own, other, *operands, taps, bias)

    sent, compact = states(False, raw, other_raw, step_bias, rate_log)
    got = swap(sent, rows)
    kept, = states(True, compact)
    corner = jax.ShapeDtypeStruct((2 * RIM, columns), BF16)
    rim_sent, rim_kept = pl.pallas_call(
        functools.partial(rim_kernel, dims),
        out_shape=(corner, corner),
        in_specs=[VMEM] * 8,
        out_specs=(VMEM, VMEM),
        compiler_params=params(4),
        name="rim_terms",
    )(ends, own, other, rim, other_rim, compact, taps, bias)
    rim_got = swap(rim_sent, rows)
    plane, far, base = pl.pallas_call(
        functools.partial(plane_kernel, state), out_shape=(packed, piece, packed_wide), in_specs=[VMEM] * 4, out_specs=(VMEM,) * 3,
        compiler_params=params(4), name="plane_total",
    )(kept, rim_kept, got, rim_got)
    parts = []
    for back in range(1, reach + 1):
        for parity in range(2):
            pairs = [
                (GROUPS * p + q, GROUPS * (p + back) + q)
                for p in range(planes - back) if p // back % 2 == parity
                for q in range(GROUPS)
            ]
            payload = far if back == reach else plane
            parts.append(swap(payload, pairs) if pairs else parts[-1])

    def whole(height, length):
        return pl.BlockSpec((height, length), lambda g: (0, 0))

    def by_group(height):
        return pl.BlockSpec((height, columns), lambda g: (0, g))

    rest = channels - inner
    bc = pl.BlockSpec((tok, rest), lambda g: (0, inner // rest))
    last = pl.BlockSpec((RIM, columns), lambda g: (tok // RIM - 1, g))
    last_bc = pl.BlockSpec((RIM, rest), lambda g: (tok // RIM - 1, inner // rest))
    a, b, c, own_state = pl.pallas_call(
        functools.partial(local_kernel, (heads, width, state, tok)),
        grid=(GROUPS,),
        out_shape=(
            jax.ShapeDtypeStruct((tok, inner), F32),
            jax.ShapeDtypeStruct((tok, inner), F32),
            jax.ShapeDtypeStruct((GROUPS, tok, state), BF16),
            jax.ShapeDtypeStruct((state + 8, inner), BF16),
        ),
        in_specs=[
            whole(*ends.shape), by_group(tok), bc, last, last_bc, by_group(RIM), pl.BlockSpec((RIM, rest), lambda g: (0, inner // rest)),
            by_group(tok), whole(tok, heads), whole(1, heads), whole(1, heads), by_group(taps_n), by_group(1),
            pl.BlockSpec((taps_n, rest), lambda g: (0, inner // rest)), pl.BlockSpec((1, rest), lambda g: (0, inner // rest)),
            whole(1, heads),
        ],
        out_specs=(by_group(tok), by_group(tok), pl.BlockSpec((GROUPS, tok, state), lambda g: (0, 0, 0)), by_group(state + 8)),
        scratch_shapes=[pltpu.VMEM((GROUPS, tok, state), BF16), pltpu.VMEM((2 * tok + 8, 3 * heads), BF16)],
        compiler_params=params(16),
        name="local_block",
        cost_estimate=pl.CostEstimate(flops=2 * 10**9, bytes_accessed=8 << 20, transcendentals=10**6),
    )(ends, own, own, other, other, rim, rim, gate_in, raw, step_bias, rate_log, taps, wide_bias,
      taps, wide_bias, skip_gain)
    prior = swap(own_state, cores)

    x0, mine = pl.pallas_call(
        functools.partial(arrive_kernel, reach, state), out_shape=(piece, piece), in_specs=[VMEM] * (1 + 2 * reach),
        out_specs=(VMEM, VMEM), compiler_params=params(4), name="arrive",
    )(base, *parts)
    x1 = swap(mine, rows)
    x2 = swap(x0, cores)
    x3 = swap(x1, cores)

    common = (a, b, c, prior, norm_gain)
    whole_out = jax.ShapeDtypeStruct((tok, inner), BF16)
    ready = [pltpu.VMEM((2, tok, columns), BF16), pltpu.SemaphoreType.DMA((2,))]
    out = pl.pallas_call(
        functools.partial(finish_near_kernel, width), out_shape=whole_out, in_specs=[VMEM] * 7, out_specs=HBM,
        scratch_shapes=ready, compiler_params=params(8), name="finish_near",
    )(*common, x0, x2)
    back_piece = pl.pallas_call(
        functools.partial(finish_back_kernel, width), out_shape=jax.ShapeDtypeStruct((tok, columns), BF16),
        in_specs=[VMEM] * 6, out_specs=VMEM, compiler_params=params(8), name="finish_back",
    )(*common, x1)
    return pl.pallas_call(
        functools.partial(finish_far_kernel, width), out_shape=whole_out, in_specs=[VMEM] * 7 + [HBM], out_specs=HBM,
        scratch_shapes=[pltpu.VMEM((tok, columns), BF16), pltpu.SemaphoreType.DMA((2,))],
        input_output_aliases={7: 0}, compiler_params=params(8), name="finish_far",
    )(*common, x3, back_piece, out)


def solution(mesh):
    split_rows = P(("groups", "seq"), None)
    return jax.shard_map(
        on_device,
        mesh=mesh,
        in_specs=(split_rows, split_rows, split_rows, P(), P(), P(), P(), P(), P(), P("groups")),
        out_specs=split_rows,
        check_vma=False,
    )
```

```python
import functools

import jax
import jax.numpy as jnp
from jax import lax
from jax.experimental import pallas as pl
from jax.experimental.pallas import tpu as pltpu
from jax.sharding import PartitionSpec as P

GROUPS = 4
PAIR = 2
RIM = 8
BLOCK = 256
EPSILON = 1e-05
F32 = jnp.float32
BF16 = jnp.bfloat16
VMEM = pl.BlockSpec(memory_space=pltpu.VMEM)
HBM = pl.BlockSpec(memory_space=pltpu.HBM)


def dot(a, b, dims=((1,), (0,))):
    return lax.dot_general(a, b, (dims, ((), ())), preferred_element_type=F32)


def silu(v):
    half = 0.5 * v
    return half + half * jnp.tanh(half)


def split(a, parts):
    out = []
    for _ in range(parts):
        top = a.astype(BF16)
        out.append(top)
        a = a - top.astype(F32)
    return out


def start_of(ends, position):
    start = jnp.zeros(position.shape, jnp.int32)
    for i in range(ends.shape[0]):
        end = ends[i : i + 1, : position.shape[1]]
        start = jnp.where(position >= end, end, start)
    return start


def start_at(ends, place):
    return start_of(ends, jnp.broadcast_to(place, (1, ends.shape[1])))


def log_sums(raw, bias, rate_log):
    v = raw.astype(F32) + bias
    step = jnp.maximum(v, 0.0) + jnp.log(1.0 + jnp.exp(-jnp.abs(v)))
    change = -jnp.exp(rate_log) * step
    down, across = (lax.broadcasted_iota(jnp.int32, (raw.shape[0],) * 2, k) for k in range(2))
    lower = jnp.where(across <= down, 1.0, 0.0).astype(BF16)
    sums = sum(dot(lower, part) for part in split(change, 3))
    return step, sums


def selector(heads, columns, width, first):
    start = (lax.broadcasted_iota(jnp.int32, (heads, 128), 0) - first) * width
    lane = lax.broadcasted_iota(jnp.int32, (heads, 128), 1)
    tiles = []
    for j in range(columns // 128):
        column = lane + j * 128
        tiles.append(jnp.where((column >= start) & (column < start + width), 1.0, 0.0))
    once = jnp.concatenate(tiles, axis=1).astype(BF16)
    return jnp.concatenate([once] * 3, axis=0)


def widen(compact, chosen):
    return dot(jnp.concatenate([p.astype(F32) for p in split(compact, 3)], axis=1).astype(BF16), chosen)


def shifts(starts, first, places, count):
    down = lax.broadcasted_iota(jnp.int32, places.shape, 0)
    inside = jnp.where(places + first >= starts[:, : places.shape[1]], 1.0, 0.0)
    back = down - places
    return jnp.concatenate([jnp.where(back == k, inside, 0.0) for k in range(count)], axis=0).astype(BF16)


def convolve(moves, rows, taps, bias):
    count = taps.shape[0]
    length = moves.shape[0] // count
    moved = dot(moves, rows)
    half = 0.5 * bias
    for back in range(count):
        half = half + (0.5 * taps[count - 1 - back : count - back]) * moved[back * length : (back + 1) * length]
    return (half + half * jnp.tanh(half)).astype(BF16)


def convolve_few(rows, reached, taps, bias):
    count = taps.shape[0]
    half = 0.5 * bias + (0.5 * taps[count - 1 :]) * rows[RIM:]
    for back in range(1, count):
        moved = pltpu.roll(rows, back, 0)[RIM:]
        half = half + (0.5 * taps[count - 1 - back : count - back]) * jnp.where(reached[back - 1], moved, 0.0)
    return (half + half * jnp.tanh(half)).astype(BF16)


def pick(first, a, b):
    return jnp.where(first, a, b)


def load_kernel(lengths, rows, raw, step_bias, rate_log, taps, bias, out_rows, rim, out_raw, out_bias, out_rate, out_taps,
                out_conv, ends, lens, sems):
    tok = rows.shape[0]
    moves = [
        (lengths, lens), (rows.at[tok - RIM :], rim), (raw, out_raw), (step_bias, out_bias), (rate_log, out_rate),
        (taps, out_taps), (bias, out_conv), (rows, out_rows),
    ]
    copies = [pltpu.make_async_copy(a, b, sems.at[k]) for k, (a, b) in enumerate(moves)]
    for copy in copies:
        copy.start()
    copies[0].wait()
    end = jnp.int32(0)
    for i in range(lengths.shape[0]):
        end = end + lens[i]
        ends[i : i + 1] = jnp.broadcast_to(end, (1, 128))
    for copy in copies[1:]:
        copy.wait()


def states_kernel(keep, dims, state, ends_ref, own, other, *rest):
    heads, width, inner, tok = dims
    if keep:
        compact, taps, bias, out, weighted = rest
    else:
        raw_own, raw_other, step_bias, rate_log, taps, bias, out, compact, weighted = rest
    index = lax.axis_index("seq")
    core, row = index % 2, (index // 2) % 2
    columns = inner // GROUPS
    wanted = row if keep else 1 - row
    group = PAIR * core + wanted
    at = pl.multiple_of(group * columns, columns)
    at_b = pl.multiple_of(inner + core * 128, 128)
    is_first = core == 0
    chip_first = (index - core) * tok
    ends = ends_ref[...]
    first_at = pick(is_first, 0, tok)
    column = lax.broadcasted_iota(jnp.int32, (2 * tok, 2 * tok), 1)
    places = jnp.where(column < tok, column + first_at, column - first_at)
    position = lax.broadcasted_iota(jnp.int32, (2 * tok, 128), 0) + chip_first
    moves = shifts(start_of(ends, position), chip_first, places, taps.shape[0])
    if not keep:
        prior = chip_first - 1
        start_a, start_b = (start_at(ends, chip_first + place)[:, :heads] for place in (tok - 1, 2 * tok - 1))
        one, two = (log_sums(raw[...], step_bias[...], rate_log[...]) for raw in (raw_own, raw_other))
        scales, lasts = [], []
        for part, start in enumerate((start_a, start_b)):
            step, sums = (pick(is_first == (part == 0), a, b) for a, b in zip(one, two))
            last = sums[tok - 1 :]
            here = position[part * tok : (part + 1) * tok, :heads] >= start
            scales.append(jnp.where(here, jnp.exp(last - sums) * step, 0.0))
            lasts.append(jnp.exp(last))
        pass_a = jnp.where(start_a <= prior, lasts[0], 0.0)
        pass_b = jnp.where(start_b <= prior + tok, lasts[1], 0.0)
        compact[:RIM] = jnp.zeros((RIM, heads), F32)
        compact[RIM:tok] = scales[0][RIM:]
        compact[tok : 2 * tok] = scales[1]
        which = lax.broadcasted_iota(jnp.int32, (8, heads), 0)
        compact[2 * tok : 2 * tok + 8] = jnp.where(which == 0, pass_b, jnp.where(which == 1, pass_a * pass_b, 0.0))
        compact[2 * tok + 8 :] = scales[0][:RIM] * pass_b
    scale = widen(compact[: 2 * tok + 8], selector(heads, columns, width, group * (heads // GROUPS)))


    def mixed(lanes_at, size):
        rows = jnp.concatenate([own[:, lanes_at], other[:, lanes_at]], axis=0)
        return convolve(moves, rows, taps[:, lanes_at], bias[lanes_at].reshape(1, size)).astype(F32)

    b_pair = mixed(pl.ds(at_b, 128), 128)
    half = b_pair.shape[1] // 2
    b_rows = pick(wanted == 0, b_pair[:, :half], b_pair[:, half:]).astype(BF16)
    for j in range(columns // BLOCK):
        lanes = slice(j * BLOCK, (j + 1) * BLOCK)
        x = mixed(pl.ds(pl.multiple_of(at + j * BLOCK, BLOCK), BLOCK), BLOCK)
        weighted[:, lanes] = (x * scale[: 2 * tok, lanes]).astype(BF16)
    state_a = dot(b_rows[:tok], weighted[:tok], ((0,), (0,)))
    state_b = dot(b_rows[tok:], weighted[tok:], ((0,), (0,)))
    passes = scale[2 * tok + 1 : 2 * tok + 2]
    total = scale[2 * tok : 2 * tok + 1] * state_a + state_b
    out[:state] = total.astype(out.dtype)
    if keep:
        out[state:] = jnp.broadcast_to(passes, (8, columns))
    else:
        out[state:] = two_rows(passes, (8, columns))


def rim_kernel(dims, ends, own, other, rim_own, rim_other, compact, taps, bias, out_sent, out_kept):
    heads, width, inner, tok = dims
    index = lax.axis_index("seq")
    core, row = index % 2, (index // 2) % 2
    columns = inner // GROUPS
    at = pl.multiple_of(PAIR * core * columns, PAIR * columns)
    at_b = pl.multiple_of(inner + core * 128, 128)
    is_first = core == 0
    chip_first = (index - core) * tok
    position = lax.broadcasted_iota(jnp.int32, (RIM, 128), 0) + chip_first
    starts = start_of(ends[...], position)
    reached = [position - back >= starts for back in range(1, taps.shape[0])]
    scale = widen(compact[2 * tok + 8 :], selector(heads, PAIR * columns, width, core * (heads // PAIR)))

    def mixed(lanes_at):
        rim = pick(is_first, rim_own[:, lanes_at].astype(F32), rim_other[:, lanes_at].astype(F32))
        top = pick(is_first, own[:RIM, lanes_at].astype(F32), other[:RIM, lanes_at].astype(F32))
        rows = jnp.concatenate([rim, top], axis=0)
        return convolve_few(rows, reached, taps[:, lanes_at], bias[lanes_at].reshape(1, 128)).astype(F32)

    b_pair = mixed(pl.ds(at_b, 128))
    half = b_pair.shape[1] // 2
    upper = row == 1
    for out, which in ((out_sent, row == 0), (out_kept, upper)):
        b_rows = pick(which, b_pair[:, half:], b_pair[:, :half])
        out[RIM:] = jnp.zeros((RIM, columns), BF16)
        out[RIM:, :half] = b_rows.astype(BF16)
    for j in range(columns // 128):
        lanes = slice(j * 128, (j + 1) * 128)
        behind = slice(columns + j * 128, columns + (j + 1) * 128)
        low = mixed(pl.ds(pl.multiple_of(at + j * 128, 128), 128)) * scale[:, lanes]
        high = mixed(pl.ds(pl.multiple_of(at + columns + j * 128, 128), 128)) * scale[:, behind]
        out_sent[:RIM, lanes] = pick(upper, low, high).astype(BF16)
        out_kept[:RIM, lanes] = pick(upper, high, low).astype(BF16)


def late(rows, state):
    return dot(rows[RIM:, :state], rows[:RIM], ((0,), (0,)))


def two_rows(passes, shape):
    top = passes.astype(BF16).astype(F32)
    which = lax.broadcasted_iota(jnp.int32, shape, 0)
    both = jnp.where(which == 0, top, jnp.where(which == 1, passes - top, 0.0))
    return both.astype(BF16)


def one_row(payload):
    wide = payload[-8:].astype(F32)
    return wide[0:1] + wide[1:2]


def plane_kernel(state, own, own_rim, got, got_rim, out, far, base):
    upper = (lax.axis_index("seq") // 2) % 2 == 1
    mine = own[:state] + late(own_rim[...], state)
    theirs = got[:state].astype(F32) + late(got_rim[...], state)
    my_pass, their_pass = own[state : state + 1], one_row(got[...])
    first, second = pick(upper, theirs, mine), pick(upper, mine, theirs)
    first_pass, later_pass = pick(upper, their_pass, my_pass), pick(upper, my_pass, their_pass)
    total = (later_pass * first + second).astype(BF16)
    out[:state] = total
    far[...] = total
    out[state:] = two_rows(my_pass * their_pass, (8, own.shape[1]))
    base[:state] = first
    base[state:] = jnp.broadcast_to(first_pass, (8, own.shape[1]))


def arrive_kernel(reach, rows, base, *rest):
    parts, (out_own, out_sent) = rest[:-2], rest[-2:]
    index = lax.axis_index("seq")
    plane = index // GROUPS
    upper = (index // 2) % 2 == 1
    state = None
    for back in range(reach, 0, -1):
        even, odd = parts[2 * (back - 1) : 2 * back]
        source = plane - back
        is_even = (source + 2 * back) // back % 2 == 0
        there = source >= 0
        arrived = jnp.where(there, pick(is_even, even[...].astype(F32), odd[...].astype(F32)), 0.0)
        if state is None:
            state = arrived[:rows]
        else:
            state = arrived[:rows] + one_row(arrived) * state
    later = base[rows : rows + 1] * state + base[:rows]
    out_own[...] = pick(upper, later, state).astype(BF16)
    out_sent[...] = pick(upper, state, later).astype(BF16)


def local_kernel(dims, ends_ref, own, other, rim, gate_hbm, raw, step_bias, rate_log, taps, bias, skip,
                 a_out, b_out, c_out, s_out, gate, sem):
    heads, width, state, tok = dims
    copy = pltpu.make_async_copy(gate_hbm, gate, sem)
    copy.start()
    index = lax.axis_index("seq")
    is_first = index % 2 == 0
    first = index * tok
    inner, per = gate.shape[1], heads // GROUPS
    columns = inner // GROUPS
    ends = ends_ref[...]
    position = lax.broadcasted_iota(jnp.int32, (tok, 128), 0) + first
    starts = start_of(ends, position)
    final = start_at(ends, first + tok - 1)
    column = lax.broadcasted_iota(jnp.int32, (tok, tok + 2 * RIM), 1)
    places = jnp.where(column < tok, column, jnp.where(column < tok + RIM, column - tok - RIM, tok))
    moves = shifts(starts, first, places, taps.shape[0])

    def mixed(lanes):
        top = pick(is_first, rim[:, lanes].astype(F32), other[tok - RIM :, lanes].astype(F32))
        extra = jnp.concatenate([top, jnp.zeros_like(top)], axis=0).astype(BF16)
        rows = jnp.concatenate([own[:, lanes], extra], axis=0)
        return convolve(moves, rows, taps[:, lanes], bias[lanes].reshape(1, lanes.stop - lanes.start)).astype(F32)

    b_all, c_all = [], []
    for j in range(2 * GROUPS * state // BLOCK):
        pieces = mixed(slice(inner + j * BLOCK, inner + (j + 1) * BLOCK))
        for k in range(BLOCK // state):
            (b_all if len(b_all) < GROUPS else c_all).append(pieces[:, k * state : (k + 1) * state].astype(BF16))
    step, sums = log_sums(raw[...], step_bias[...], rate_log[...])
    ending_decay = jnp.exp(sums[tok - 1 :])
    passed = jnp.where(final[:, :heads] < first, ending_decay, 0.0)
    rest = jnp.concatenate([ending_decay, passed, skip[...], jnp.zeros((5, heads), F32)], axis=0)
    whole = jnp.concatenate([jnp.exp(sums), jnp.exp(-sums) * step, rest], axis=0)
    chosen = selector(per, columns, width, 0)
    down, across = (lax.broadcasted_iota(jnp.int32, (tok, tok), k) for k in range(2))
    causal = (down >= across) & (across + first >= starts[:, :tok])
    here = position[:, :state] >= final[:, :state]
    entered = jnp.concatenate([starts] * (BLOCK // 128), axis=1) < first
    copy.wait()
    for g in range(GROUPS):
        wide = widen(whole[:, g * per : (g + 1) * per], chosen)
        b_rows, c_rows = b_all[g], c_all[g]
        c_out[g] = c_rows
        mask = jnp.where(causal, dot(c_rows, b_rows, ((1,), (1,))), 0.0)
        m_top, m_rest = split(mask, 2)
        lhs = jnp.concatenate([m_top.astype(F32), m_rest.astype(F32)], axis=1).astype(BF16)
        ending = jnp.where(here, b_rows.astype(F32), 0.0).astype(BF16)
        for j in range(columns // BLOCK):
            part = slice(j * BLOCK, (j + 1) * BLOCK)
            lanes = slice(g * columns + j * BLOCK, g * columns + (j + 1) * BLOCK)
            inward, outward = wide[:tok, part], wide[tok : 2 * tok, part]
            end_decay, gain = wide[2 * tok : 2 * tok + 1, part], wide[2 * tok + 2 : 2 * tok + 3, part]
            x = mixed(lanes)
            s_top, s_rest = split(x * outward, 2)
            within = dot(lhs, jnp.concatenate([s_top, s_top], axis=0)) + dot(m_top, s_rest)
            local = dot(ending, s_top, ((0,), (0,))) + dot(ending, s_rest, ((0,), (0,)))
            opened = silu(gate[:, lanes].astype(F32))
            a_out[:, lanes] = (inward * within + gain * x) * opened
            b_out[:, lanes] = jnp.where(entered, inward * opened, 0.0)
            s_out[:state, lanes] = (end_decay * local).astype(BF16)
        s_out[state:, g * columns : (g + 1) * columns] = two_rows(wide[2 * tok + 1 : 2 * tok + 2], (8, columns))


def place_of(far_core, far_row):
    index = lax.axis_index("seq")
    core, row = index % 2, (index // 2) % 2
    return PAIR * (1 - core if far_core else core) + (1 - row if far_row else row)


def finish_piece(width, group, arrived, a_ref, b_ref, c_ref, prior, gain, put):
    second = lax.axis_index("seq") % 2 == 1
    state_rows, columns = arrived.shape
    block = BLOCK
    down, across = (lax.broadcasted_iota(jnp.int32, (block, block), k) for k in range(2))
    low = across - lax.rem(across, width)
    means = jnp.where((down >= low) & (down < low + width), 1.0 / width, 0.0).astype(BF16)
    c_rows = c_ref[group]
    for j in range(columns // block):
        lanes = slice(j * block, (j + 1) * block)
        at = pl.ds(pl.multiple_of(group * columns + j * block, block), block)
        state = arrived[:, lanes].astype(F32)
        before = prior[:, at].astype(F32)
        stepped = (before[state_rows : state_rows + 1] + before[state_rows + 1 : state_rows + 2]) * state + before[:state_rows]
        state = pick(second, stepped, state).astype(BF16)
        gated = a_ref[:, at] + b_ref[:, at] * dot(c_rows, state)
        mean = dot((gated * gated).astype(BF16), means)
        put(lanes, (gated * lax.rsqrt(mean + EPSILON) * gain[:, at]).astype(BF16))


def finish_near_kernel(width, a, b, c, prior, gain, x0, x2, out, ready, sems):
    columns, copies = x0.shape[1], []
    for k, arrived in enumerate((x0, x2)):
        group = place_of(k == 1, False)

        def put(lanes, value, k=k):
            ready[k, :, lanes] = value

        finish_piece(width, group, arrived, a, b, c, prior, gain, put)
        target = out.at[:, pl.ds(pl.multiple_of(group * columns, columns), columns)]
        copies.append(pltpu.make_async_copy(ready.at[k], target, sems.at[k]))
        copies[-1].start()
    for copy in copies:
        copy.wait()


def finish_back_kernel(width, a, b, c, prior, gain, x1, out):
    def put(lanes, value):
        out[:, lanes] = value

    finish_piece(width, place_of(False, True), x1, a, b, c, prior, gain, put)


def finish_far_kernel(width, a, b, c, prior, gain, x3, piece, begun, out, ready, sems):
    columns = x3.shape[1]

    def target(group):
        return out.at[:, pl.ds(pl.multiple_of(group * columns, columns), columns)]

    early = pltpu.make_async_copy(piece, target(place_of(False, True)), sems.at[0])
    early.start()

    def put(lanes, value):
        ready[:, lanes] = value

    group = place_of(True, True)
    finish_piece(width, group, x3, a, b, c, prior, gain, put)
    copy = pltpu.make_async_copy(ready, target(group), sems.at[1])
    copy.start()
    early.wait()
    copy.wait()


def swap(block, pairs):
    return lax.ppermute(block, "seq", [*pairs, *((b, a) for a, b in pairs)])


def on_device(mixer_in, gate_in, step_raw, step_bias, rate_log, conv_weight, conv_bias, skip_gain, norm_gain, doc_lengths):
    tok, channels = mixer_in.shape
    heads, inner = rate_log.shape[0], gate_in.shape[1]
    width = inner // heads
    state = (channels - inner) // (2 * GROUPS)
    devices = lax.axis_size("seq")
    planes = devices // GROUPS
    columns = inner // GROUPS
    taps_n = conv_weight.shape[0]
    longest = devices * tok // 2
    reach = -(-(longest - 1) // (GROUPS * tok))
    row = lambda a: a.reshape(1, -1)
    step_bias, rate_log, skip_gain, norm_gain = map(row, (step_bias, rate_log, skip_gain, norm_gain))
    cores = [(i, i + 1) for i in range(0, devices, 2)]
    rows = [(i, i + 2) for i in range(0, devices, 4) for i in (i, i + 1)]
    chips = [(i, i + 1) for i in range(1, devices - 1, 2)]

    def hbm(block):
        return pltpu.with_memory_space_constraint(block, pltpu.HBM)

    other = swap(mixer_in, cores)
    other_raw = swap(step_raw, cores)
    own, rim, raw, step_bias, rate_log, taps, bias, ends = pl.pallas_call(
        load_kernel,
        out_shape=(
            jax.ShapeDtypeStruct((tok, channels), BF16), jax.ShapeDtypeStruct((RIM, channels), BF16),
            jax.ShapeDtypeStruct((tok, heads), BF16), jax.ShapeDtypeStruct((1, heads), F32),
            jax.ShapeDtypeStruct((1, heads), F32), jax.ShapeDtypeStruct((taps_n, channels), F32),
            jax.ShapeDtypeStruct((channels,), F32), jax.ShapeDtypeStruct((doc_lengths.shape[0], 128), jnp.int32),
        ),
        in_specs=[HBM] * 7,
        out_specs=(VMEM,) * 8,
        scratch_shapes=[pltpu.SMEM(doc_lengths.shape, jnp.int32), pltpu.SemaphoreType.DMA((8,))],
        compiler_params=pltpu.CompilerParams(vmem_limit_bytes=4 << 20),
        name="load",
    )(*map(hbm, (doc_lengths, mixer_in, step_raw, step_bias, rate_log, conv_weight, conv_bias)))
    rim = swap(rim, chips)
    other_rim = swap(rim, cores)

    def params(mib):
        return pltpu.CompilerParams(vmem_limit_bytes=mib << 20)

    packed = jax.ShapeDtypeStruct((state + 8, columns), BF16)
    packed_wide = jax.ShapeDtypeStruct((state + 8, columns), F32)
    piece = jax.ShapeDtypeStruct((state, columns), BF16)
    dims = (heads, width, inner, tok)

    def states(keep, *operands):
        compact = () if keep else (jax.ShapeDtypeStruct((2 * tok + 16, heads), F32),)
        return pl.pallas_call(
            functools.partial(states_kernel, keep, dims, state),
            out_shape=(packed_wide if keep else packed, *compact),
            in_specs=[VMEM] * (3 + len(operands) + 2),
            out_specs=(VMEM,) * (1 + len(compact)),
            scratch_shapes=[pltpu.VMEM((2 * tok, columns), BF16)],
            compiler_params=params(8),
            name="states_kept" if keep else "states_sent",
        )(ends, own, other, *operands, taps, bias)

    sent, compact = states(False, raw, other_raw, step_bias, rate_log)
    got = swap(sent, rows)
    kept, = states(True, compact)
    corner = jax.ShapeDtypeStruct((2 * RIM, columns), BF16)
    rim_sent, rim_kept = pl.pallas_call(
        functools.partial(rim_kernel, dims),
        out_shape=(corner, corner),
        in_specs=[VMEM] * 8,
        out_specs=(VMEM, VMEM),
        compiler_params=params(4),
        name="rim_terms",
    )(ends, own, other, rim, other_rim, compact, taps, bias)
    rim_got = swap(rim_sent, rows)
    plane, far, base = pl.pallas_call(
        functools.partial(plane_kernel, state), out_shape=(packed, piece, packed_wide), in_specs=[VMEM] * 4, out_specs=(VMEM,) * 3,
        compiler_params=params(4), name="plane_total",
    )(kept, rim_kept, got, rim_got)
    parts = []
    for back in range(1, reach + 1):
        for parity in range(2):
            pairs = [
                (GROUPS * p + q, GROUPS * (p + back) + q)
                for p in range(planes - back) if p // back % 2 == parity
                for q in range(GROUPS)
            ]
            payload = far if back == reach else plane
            parts.append(swap(payload, pairs) if pairs else parts[-1])

    a, b, c, own_state = pl.pallas_call(
        functools.partial(local_kernel, (heads, width, state, tok)),
        out_shape=(
            jax.ShapeDtypeStruct((tok, inner), F32),
            jax.ShapeDtypeStruct((tok, inner), F32),
            jax.ShapeDtypeStruct((GROUPS, tok, state), BF16),
            jax.ShapeDtypeStruct((state + 8, inner), BF16),
        ),
        in_specs=[VMEM] * 4 + [HBM] + [VMEM] * 6,
        out_specs=(VMEM,) * 4,
        scratch_shapes=[pltpu.VMEM((tok, inner), BF16), pltpu.SemaphoreType.DMA],
        compiler_params=params(16),
        name="local_block",
    )(ends, own, other, rim, hbm(gate_in), raw, step_bias, rate_log, taps, bias, skip_gain)
    prior = swap(own_state, cores)

    x0, mine = pl.pallas_call(
        functools.partial(arrive_kernel, reach, state), out_shape=(piece, piece), in_specs=[VMEM] * (1 + 2 * reach),
        out_specs=(VMEM, VMEM), compiler_params=params(4), name="arrive",
    )(base, *parts)
    x1 = swap(mine, rows)
    x2 = swap(x0, cores)
    x3 = swap(x1, cores)

    common = (a, b, c, prior, norm_gain)
    whole_out = jax.ShapeDtypeStruct((tok, inner), BF16)
    ready = [pltpu.VMEM((2, tok, columns), BF16), pltpu.SemaphoreType.DMA((2,))]
    out = pl.pallas_call(
        functools.partial(finish_near_kernel, width), out_shape=whole_out, in_specs=[VMEM] * 7, out_specs=HBM,
        scratch_shapes=ready, compiler_params=params(8), name="finish_near",
    )(*common, x0, x2)
    back_piece = pl.pallas_call(
        functools.partial(finish_back_kernel, width), out_shape=jax.ShapeDtypeStruct((tok, columns), BF16),
        in_specs=[VMEM] * 6, out_specs=VMEM, compiler_params=params(8), name="finish_back",
    )(*common, x1)
    return pl.pallas_call(
        functools.partial(finish_far_kernel, width), out_shape=whole_out, in_specs=[VMEM] * 7 + [HBM], out_specs=HBM,
        scratch_shapes=[pltpu.VMEM((tok, columns), BF16), pltpu.SemaphoreType.DMA((2,))],
        input_output_aliases={7: 0}, compiler_params=params(8), name="finish_far",
    )(*common, x3, back_piece, out)


def solution(mesh):
    split_rows = P(("groups", "seq"), None)
    return jax.shard_map(
        on_device,
        mesh=mesh,
        in_specs=(split_rows, split_rows, split_rows, P(), P(), P(), P(), P(), P(), P("groups")),
        out_specs=split_rows,
        check_vma=False,
    )
```

```python
import functools

import jax
import jax.numpy as jnp
from jax import lax
from jax.experimental import pallas as pl
from jax.experimental.pallas import tpu as pltpu
from jax.sharding import PartitionSpec as P

GROUPS = 4
PAIR = 2
RIM = 8
BLOCK = 256
EPSILON = 1e-05
F32 = jnp.float32
BF16 = jnp.bfloat16
VMEM = pl.BlockSpec(memory_space=pltpu.VMEM)
HBM = pl.BlockSpec(memory_space=pltpu.HBM)


def dot(a, b, dims=((1,), (0,))):
    return lax.dot_general(a, b, (dims, ((), ())), preferred_element_type=F32)


def silu(v):
    half = 0.5 * v
    return half + half * jnp.tanh(half)


def split(a, parts):
    out = []
    for _ in range(parts):
        top = a.astype(BF16)
        out.append(top)
        a = a - top.astype(F32)
    return out


def start_of(ends, position):
    start = jnp.zeros(position.shape, jnp.int32)
    for i in range(ends.shape[0]):
        end = ends[i : i + 1, : position.shape[1]]
        start = jnp.where(position >= end, end, start)
    return start


def start_at(ends, place):
    return start_of(ends, jnp.broadcast_to(place, (1, ends.shape[1])))


def log_sums(raw, bias, rate_log):
    v = raw.astype(F32) + bias
    step = jnp.maximum(v, 0.0) + jnp.log(1.0 + jnp.exp(-jnp.abs(v)))
    change = -jnp.exp(rate_log) * step
    down, across = (lax.broadcasted_iota(jnp.int32, (raw.shape[0],) * 2, k) for k in range(2))
    lower = jnp.where(across <= down, 1.0, 0.0).astype(BF16)
    sums = sum(dot(lower, part) for part in split(change, 3))
    return step, sums


def selector(heads, columns, width, first):
    start = (lax.broadcasted_iota(jnp.int32, (heads, 128), 0) - first) * width
    lane = lax.broadcasted_iota(jnp.int32, (heads, 128), 1)
    tiles = []
    for j in range(columns // 128):
        column = lane + j * 128
        tiles.append(jnp.where((column >= start) & (column < start + width), 1.0, 0.0))
    once = jnp.concatenate(tiles, axis=1).astype(BF16)
    return jnp.concatenate([once] * 3, axis=0)


def widen(compact, chosen):
    return dot(jnp.concatenate([p.astype(F32) for p in split(compact, 3)], axis=1).astype(BF16), chosen)


def shifts(starts, first, places, count):
    down = lax.broadcasted_iota(jnp.int32, places.shape, 0)
    inside = jnp.where(places + first >= starts[:, : places.shape[1]], 1.0, 0.0)
    back = down - places
    return jnp.concatenate([jnp.where(back == k, inside, 0.0) for k in range(count)], axis=0).astype(BF16)


def convolve(moves, rows, taps, bias):
    count = taps.shape[0]
    length = moves.shape[0] // count
    moved = dot(moves, rows)
    half = 0.5 * bias
    for back in range(count):
        half = half + (0.5 * taps[count - 1 - back : count - back]) * moved[back * length : (back + 1) * length]
    return (half + half * jnp.tanh(half)).astype(BF16)


def convolve_few(rows, reached, taps, bias):
    count = taps.shape[0]
    half = 0.5 * bias + (0.5 * taps[count - 1 :]) * rows[RIM:]
    for back in range(1, count):
        moved = pltpu.roll(rows, back, 0)[RIM:]
        half = half + (0.5 * taps[count - 1 - back : count - back]) * jnp.where(reached[back - 1], moved, 0.0)
    return (half + half * jnp.tanh(half)).astype(BF16)


def pick(first, a, b):
    return jnp.where(first, a, b)


def load_kernel(dims, lengths, rows, raw, step_bias, rate_log, taps, bias, out_rows, packed, out_raw, out_bias, out_rate, out_taps,
                out_conv, ends, lens, rim, sems):
    tok = rows.shape[0]
    inner, pair = dims
    moves = [
        (lengths, lens), (rows.at[tok - RIM :], rim), (raw, out_raw), (step_bias, out_bias), (rate_log, out_rate),
        (taps, out_taps), (bias, out_conv), (rows, out_rows),
    ]
    copies = [pltpu.make_async_copy(a, b, sems.at[k]) for k, (a, b) in enumerate(moves)]
    for copy in copies:
        copy.start()
    copies[0].wait()
    end = jnp.int32(0)
    for i in range(lengths.shape[0]):
        end = end + lens[i]
        ends[i : i + 1] = jnp.broadcast_to(end, (1, 128))
    copies[1].wait()
    segments = []
    for k in range(PAIR):
        starts = ((k * inner // PAIR, inner // PAIR), (inner + k * pair, pair), (inner + (PAIR + k) * pair, pair))
        segments.append(jnp.concatenate([rim[:, a : a + n].astype(F32) for a, n in starts], axis=1))
    down = lax.broadcasted_iota(jnp.int32, segments[0].shape, 0)
    mixed = jnp.where(down < 3, pltpu.roll(segments[0], 3, 0), pltpu.roll(segments[1], 6, 0))
    packed[...] = mixed.astype(BF16)
    for copy in copies[2:]:
        copy.wait()


def unpacked(packed, lanes, second):
    rows = packed[:, lanes].astype(F32)
    return pick(second, pltpu.roll(rows, 2, 0), pltpu.roll(rows, 5, 0))


def states_kernel(keep, dims, state, ends_ref, own, other, *rest):
    heads, width, inner, tok = dims
    if keep:
        compact, taps, bias, out, weighted = rest
    else:
        raw_own, raw_other, step_bias, rate_log, taps, bias, out, compact, weighted = rest
    index = lax.axis_index("seq")
    core, row = index % 2, (index // 2) % 2
    columns = inner // GROUPS
    wanted = row if keep else 1 - row
    group = PAIR * core + wanted
    at = pl.multiple_of(group * columns, columns)
    at_b = pl.multiple_of(inner + core * 128, 128)
    is_first = core == 0
    chip_first = (index - core) * tok
    ends = ends_ref[...]
    first_at = pick(is_first, 0, tok)
    column = lax.broadcasted_iota(jnp.int32, (2 * tok, 2 * tok), 1)
    places = jnp.where(column < tok, column + first_at, column - first_at)
    position = lax.broadcasted_iota(jnp.int32, (2 * tok, 128), 0) + chip_first
    moves = shifts(start_of(ends, position), chip_first, places, taps.shape[0])
    if not keep:
        prior = chip_first - 1
        start_a, start_b = (start_at(ends, chip_first + place)[:, :heads] for place in (tok - 1, 2 * tok - 1))
        one, two = (log_sums(raw[...], step_bias[...], rate_log[...]) for raw in (raw_own, raw_other))
        scales, lasts = [], []
        for part, start in enumerate((start_a, start_b)):
            step, sums = (pick(is_first == (part == 0), a, b) for a, b in zip(one, two))
            last = sums[tok - 1 :]
            here = position[part * tok : (part + 1) * tok, :heads] >= start
            scales.append(jnp.where(here, jnp.exp(last - sums) * step, 0.0))
            lasts.append(jnp.exp(last))
        pass_a = jnp.where(start_a <= prior, lasts[0], 0.0)
        pass_b = jnp.where(start_b <= prior + tok, lasts[1], 0.0)
        compact[:RIM] = jnp.zeros((RIM, heads), F32)
        compact[RIM:tok] = scales[0][RIM:]
        compact[tok : 2 * tok] = scales[1]
        which = lax.broadcasted_iota(jnp.int32, (8, heads), 0)
        compact[2 * tok : 2 * tok + 8] = jnp.where(which == 0, pass_b, jnp.where(which == 1, pass_a * pass_b, 0.0))
        compact[2 * tok + 8 :] = scales[0][:RIM] * pass_b
    scale = widen(compact[: 2 * tok + 8], selector(heads, columns, width, group * (heads // GROUPS)))


    def mixed(lanes_at, size):
        rows = jnp.concatenate([own[:, lanes_at], other[:, lanes_at]], axis=0)
        return convolve(moves, rows, taps[:, lanes_at], bias[lanes_at].reshape(1, size)).astype(F32)

    b_pair = mixed(pl.ds(at_b, 128), 128)
    half = b_pair.shape[1] // 2
    b_rows = pick(wanted == 0, b_pair[:, :half], b_pair[:, half:]).astype(BF16)
    for j in range(columns // BLOCK):
        lanes = slice(j * BLOCK, (j + 1) * BLOCK)
        x = mixed(pl.ds(pl.multiple_of(at + j * BLOCK, BLOCK), BLOCK), BLOCK)
        weighted[:, lanes] = (x * scale[: 2 * tok, lanes]).astype(BF16)
    state_a = dot(b_rows[:tok], weighted[:tok], ((0,), (0,)))
    state_b = dot(b_rows[tok:], weighted[tok:], ((0,), (0,)))
    passes = scale[2 * tok + 1 : 2 * tok + 2]
    total = scale[2 * tok : 2 * tok + 1] * state_a + state_b
    out[:state] = total.astype(out.dtype)
    if keep:
        out[state:] = jnp.broadcast_to(passes, (8, columns))
    else:
        out[state:] = two_rows(passes, (8, columns))


def rim_kernel(dims, ends, own, other, rim_own, rim_other, compact, taps, bias, out_sent, out_kept):
    heads, width, inner, tok = dims
    index = lax.axis_index("seq")
    core, row = index % 2, (index // 2) % 2
    columns = inner // GROUPS
    at = pl.multiple_of(PAIR * core * columns, PAIR * columns)
    at_b = pl.multiple_of(inner + core * 128, 128)
    is_first = core == 0
    chip_first = (index - core) * tok
    position = lax.broadcasted_iota(jnp.int32, (RIM, 128), 0) + chip_first
    starts = start_of(ends[...], position)
    reached = [position - back >= starts for back in range(1, taps.shape[0])]
    scale = widen(compact[2 * tok + 8 :], selector(heads, PAIR * columns, width, core * (heads // PAIR)))

    def mixed(lanes_at, lanes):
        rim = pick(is_first, unpacked(rim_own, lanes, False), unpacked(rim_other, lanes, True))
        top = pick(is_first, own[:RIM, lanes_at].astype(F32), other[:RIM, lanes_at].astype(F32))
        rows = jnp.concatenate([rim, top], axis=0)
        return convolve_few(rows, reached, taps[:, lanes_at], bias[lanes_at].reshape(1, 128)).astype(F32)

    b_pair = mixed(pl.ds(at_b, 128), slice(PAIR * columns, PAIR * columns + 128))
    half = b_pair.shape[1] // 2
    upper = row == 1
    for out, which in ((out_sent, row == 0), (out_kept, upper)):
        b_rows = pick(which, b_pair[:, half:], b_pair[:, :half])
        out[:, columns:] = jnp.concatenate([b_rows, jnp.zeros_like(b_rows)], axis=1).astype(BF16)
    for j in range(columns // 128):
        lanes = slice(j * 128, (j + 1) * 128)
        behind = slice(columns + j * 128, columns + (j + 1) * 128)
        low = mixed(pl.ds(pl.multiple_of(at + j * 128, 128), 128), lanes) * scale[:, lanes]
        high = mixed(pl.ds(pl.multiple_of(at + columns + j * 128, 128), 128), behind) * scale[:, behind]
        out_sent[:, lanes] = pick(upper, low, high).astype(BF16)
        out_kept[:, lanes] = pick(upper, high, low).astype(BF16)


def late(rows, state, columns):
    return dot(rows[:, columns : columns + state], rows[:, :columns], ((0,), (0,)))


def two_rows(passes, shape):
    top = passes.astype(BF16).astype(F32)
    which = lax.broadcasted_iota(jnp.int32, shape, 0)
    both = jnp.where(which == 0, top, jnp.where(which == 1, passes - top, 0.0))
    return both.astype(BF16)


def one_row(payload):
    wide = payload[-8:].astype(F32)
    return wide[0:1] + wide[1:2]


def plane_kernel(state, own, own_rim, got, got_rim, out, far, base):
    upper = (lax.axis_index("seq") // 2) % 2 == 1
    mine = own[:state] + late(own_rim[...], state, own.shape[1])
    theirs = got[:state].astype(F32) + late(got_rim[...], state, own.shape[1])
    my_pass, their_pass = own[state : state + 1], one_row(got[...])
    first, second = pick(upper, theirs, mine), pick(upper, mine, theirs)
    first_pass, later_pass = pick(upper, their_pass, my_pass), pick(upper, my_pass, their_pass)
    total = (later_pass * first + second).astype(BF16)
    out[:state] = total
    far[...] = total
    out[state:] = two_rows(my_pass * their_pass, (8, own.shape[1]))
    base[:state] = first
    base[state:] = jnp.broadcast_to(first_pass, (8, own.shape[1]))


def arrive_kernel(reach, rows, base, *rest):
    parts, (out_own, out_sent) = rest[:-2], rest[-2:]
    index = lax.axis_index("seq")
    plane = index // GROUPS
    upper = (index // 2) % 2 == 1
    state = None
    for back in range(reach, 0, -1):
        even, odd = parts[2 * (back - 1) : 2 * back]
        source = plane - back
        is_even = (source + 2 * back) // back % 2 == 0
        there = source >= 0
        arrived = jnp.where(there, pick(is_even, even[...].astype(F32), odd[...].astype(F32)), 0.0)
        if state is None:
            state = arrived[:rows]
        else:
            state = arrived[:rows] + one_row(arrived) * state
    later = base[rows : rows + 1] * state + base[:rows]
    out_own[...] = pick(upper, later, state).astype(BF16)
    out_sent[...] = pick(upper, state, later).astype(BF16)


def local_kernel(dims, ends_ref, own, other, rim, gate_hbm, raw, step_bias, rate_log, taps, bias, skip,
                 a_out, b_out, c_out, s_out, gate, sem):
    heads, width, state, tok = dims
    copy = pltpu.make_async_copy(gate_hbm, gate, sem)
    copy.start()
    index = lax.axis_index("seq")
    is_first = index % 2 == 0
    first = index * tok
    inner, per = gate.shape[1], heads // GROUPS
    columns = inner // GROUPS
    ends = ends_ref[...]
    position = lax.broadcasted_iota(jnp.int32, (tok, 128), 0) + first
    starts = start_of(ends, position)
    final = start_at(ends, first + tok - 1)
    column = lax.broadcasted_iota(jnp.int32, (tok, tok + 2 * RIM), 1)
    places = jnp.where(column < tok, column, jnp.where(column < tok + RIM, column - tok - RIM, tok))
    moves = shifts(starts, first, places, taps.shape[0])

    def rim_rows(lanes):
        if lanes.start < inner:
            second, at = divmod(lanes.start, inner // PAIR)
            return unpacked(rim, slice(at, at + BLOCK), second == 1)
        at = inner // PAIR + (lanes.start - inner) // PAIR
        halves = [unpacked(rim, slice(at, at + BLOCK // PAIR), k == 1) for k in range(PAIR)]
        return jnp.concatenate(halves, axis=1)

    def mixed(lanes):
        top = pick(is_first, rim_rows(lanes), other[tok - RIM :, lanes].astype(F32))
        extra = jnp.concatenate([top, jnp.zeros_like(top)], axis=0).astype(BF16)
        rows = jnp.concatenate([own[:, lanes], extra], axis=0)
        return convolve(moves, rows, taps[:, lanes], bias[lanes].reshape(1, lanes.stop - lanes.start)).astype(F32)

    b_all, c_all = [], []
    for j in range(2 * GROUPS * state // BLOCK):
        pieces = mixed(slice(inner + j * BLOCK, inner + (j + 1) * BLOCK))
        for k in range(BLOCK // state):
            (b_all if len(b_all) < GROUPS else c_all).append(pieces[:, k * state : (k + 1) * state].astype(BF16))
    step, sums = log_sums(raw[...], step_bias[...], rate_log[...])
    ending_decay = jnp.exp(sums[tok - 1 :])
    passed = jnp.where(final[:, :heads] < first, ending_decay, 0.0)
    rest = jnp.concatenate([ending_decay, passed, skip[...], jnp.zeros((5, heads), F32)], axis=0)
    whole = jnp.concatenate([jnp.exp(sums), jnp.exp(-sums) * step, rest], axis=0)
    chosen = selector(per, columns, width, 0)
    down, across = (lax.broadcasted_iota(jnp.int32, (tok, tok), k) for k in range(2))
    causal = (down >= across) & (across + first >= starts[:, :tok])
    here = position[:, :state] >= final[:, :state]
    entered = jnp.concatenate([starts] * (BLOCK // 128), axis=1) < first
    copy.wait()
    for g in range(GROUPS):
        wide = widen(whole[:, g * per : (g + 1) * per], chosen)
        b_rows, c_rows = b_all[g], c_all[g]
        c_out[g] = c_rows
        mask = jnp.where(causal, dot(c_rows, b_rows, ((1,), (1,))), 0.0)
        m_top, m_rest = split(mask, 2)
        lhs = jnp.concatenate([m_top.astype(F32), m_rest.astype(F32)], axis=1).astype(BF16)
        ending = jnp.where(here, b_rows.astype(F32), 0.0).astype(BF16)
        for j in range(columns // BLOCK):
            part = slice(j * BLOCK, (j + 1) * BLOCK)
            lanes = slice(g * columns + j * BLOCK, g * columns + (j + 1) * BLOCK)
            inward, outward = wide[:tok, part], wide[tok : 2 * tok, part]
            end_decay, gain = wide[2 * tok : 2 * tok + 1, part], wide[2 * tok + 2 : 2 * tok + 3, part]
            x = mixed(lanes)
            s_top, s_rest = split(x * outward, 2)
            within = dot(lhs, jnp.concatenate([s_top, s_top], axis=0)) + dot(m_top, s_rest)
            local = dot(ending, s_top, ((0,), (0,))) + dot(ending, s_rest, ((0,), (0,)))
            opened = silu(gate[:, lanes].astype(F32))
            a_out[:, lanes] = (inward * within + gain * x) * opened
            b_out[:, lanes] = jnp.where(entered, inward * opened, 0.0)
            s_out[:state, lanes] = (end_decay * local).astype(BF16)
        s_out[state:, g * columns : (g + 1) * columns] = two_rows(wide[2 * tok + 1 : 2 * tok + 2], (8, columns))


def place_of(far_core, far_row):
    index = lax.axis_index("seq")
    core, row = index % 2, (index // 2) % 2
    return PAIR * (1 - core if far_core else core) + (1 - row if far_row else row)


def finish_piece(width, group, arrived, a_ref, b_ref, c_ref, prior, gain, put):
    second = lax.axis_index("seq") % 2 == 1
    state_rows, columns = arrived.shape
    block = BLOCK
    down, across = (lax.broadcasted_iota(jnp.int32, (block, block), k) for k in range(2))
    low = across - lax.rem(across, width)
    means = jnp.where((down >= low) & (down < low + width), 1.0 / width, 0.0).astype(BF16)
    c_rows = c_ref[group]
    for j in range(columns // block):
        lanes = slice(j * block, (j + 1) * block)
        at = pl.ds(pl.multiple_of(group * columns + j * block, block), block)
        state = arrived[:, lanes].astype(F32)
        before = prior[:, at].astype(F32)
        stepped = (before[state_rows : state_rows + 1] + before[state_rows + 1 : state_rows + 2]) * state + before[:state_rows]
        state = pick(second, stepped, state).astype(BF16)
        gated = a_ref[:, at] + b_ref[:, at] * dot(c_rows, state)
        mean = dot((gated * gated).astype(BF16), means)
        put(lanes, (gated * lax.rsqrt(mean + EPSILON) * gain[:, at]).astype(BF16))


def finish_near_kernel(width, a, b, c, prior, gain, x0, x2, out, ready, sems):
    columns, copies = x0.shape[1], []
    for k, arrived in enumerate((x0, x2)):
        group = place_of(k == 1, False)

        def put(lanes, value, k=k):
            ready[k, :, lanes] = value

        finish_piece(width, group, arrived, a, b, c, prior, gain, put)
        target = out.at[:, pl.ds(pl.multiple_of(group * columns, columns), columns)]
        copies.append(pltpu.make_async_copy(ready.at[k], target, sems.at[k]))
        copies[-1].start()
    for copy in copies:
        copy.wait()


def finish_back_kernel(width, a, b, c, prior, gain, x1, out):
    def put(lanes, value):
        out[:, lanes] = value

    finish_piece(width, place_of(False, True), x1, a, b, c, prior, gain, put)


def finish_far_kernel(width, a, b, c, prior, gain, x3, piece, begun, out, ready, sems):
    columns = x3.shape[1]

    def target(group):
        return out.at[:, pl.ds(pl.multiple_of(group * columns, columns), columns)]

    early = pltpu.make_async_copy(piece, target(place_of(False, True)), sems.at[0])
    early.start()

    def put(lanes, value):
        ready[:, lanes] = value

    group = place_of(True, True)
    finish_piece(width, group, x3, a, b, c, prior, gain, put)
    copy = pltpu.make_async_copy(ready, target(group), sems.at[1])
    copy.start()
    early.wait()
    copy.wait()


def swap(block, pairs):
    return lax.ppermute(block, "seq", [*pairs, *((b, a) for a, b in pairs)])


def on_device(mixer_in, gate_in, step_raw, step_bias, rate_log, conv_weight, conv_bias, skip_gain, norm_gain, doc_lengths):
    tok, channels = mixer_in.shape
    heads, inner = rate_log.shape[0], gate_in.shape[1]
    width = inner // heads
    state = (channels - inner) // (2 * GROUPS)
    devices = lax.axis_size("seq")
    planes = devices // GROUPS
    columns = inner // GROUPS
    taps_n = conv_weight.shape[0]
    longest = devices * tok // 2
    reach = -(-(longest - 1) // (GROUPS * tok))
    row = lambda a: a.reshape(1, -1)
    step_bias, rate_log, skip_gain, norm_gain = map(row, (step_bias, rate_log, skip_gain, norm_gain))
    cores = [(i, i + 1) for i in range(0, devices, 2)]
    rows = [(i, i + 2) for i in range(0, devices, 4) for i in (i, i + 1)]
    chips = [(i, i + 1) for i in range(1, devices - 1, 2)]

    def hbm(block):
        return pltpu.with_memory_space_constraint(block, pltpu.HBM)

    other = swap(mixer_in, cores)
    other_raw = swap(step_raw, cores)
    own, rim, raw, step_bias, rate_log, taps, bias, ends = pl.pallas_call(
        functools.partial(load_kernel, (inner, PAIR * state)),
        out_shape=(
            jax.ShapeDtypeStruct((tok, channels), BF16), jax.ShapeDtypeStruct((RIM, channels // PAIR), BF16),
            jax.ShapeDtypeStruct((tok, heads), BF16), jax.ShapeDtypeStruct((1, heads), F32),
            jax.ShapeDtypeStruct((1, heads), F32), jax.ShapeDtypeStruct((taps_n, channels), F32),
            jax.ShapeDtypeStruct((channels,), F32), jax.ShapeDtypeStruct((doc_lengths.shape[0], 128), jnp.int32),
        ),
        in_specs=[HBM] * 7,
        out_specs=(VMEM,) * 8,
        scratch_shapes=[pltpu.SMEM(doc_lengths.shape, jnp.int32), pltpu.VMEM((RIM, channels), BF16), pltpu.SemaphoreType.DMA((8,))],
        compiler_params=pltpu.CompilerParams(vmem_limit_bytes=4 << 20),
        name="load",
    )(*map(hbm, (doc_lengths, mixer_in, step_raw, step_bias, rate_log, conv_weight, conv_bias)))
    rim = swap(rim, chips)
    other_rim = swap(rim, cores)

    def params(mib):
        return pltpu.CompilerParams(vmem_limit_bytes=mib << 20)

    packed = jax.ShapeDtypeStruct((state + 8, columns), BF16)
    packed_wide = jax.ShapeDtypeStruct((state + 8, columns), F32)
    piece = jax.ShapeDtypeStruct((state, columns), BF16)
    dims = (heads, width, inner, tok)

    def states(keep, *operands):
        compact = () if keep else (jax.ShapeDtypeStruct((2 * tok + 16, heads), F32),)
        return pl.pallas_call(
            functools.partial(states_kernel, keep, dims, state),
            out_shape=(packed_wide if keep else packed, *compact),
            in_specs=[VMEM] * (3 + len(operands) + 2),
            out_specs=(VMEM,) * (1 + len(compact)),
            scratch_shapes=[pltpu.VMEM((2 * tok, columns), BF16)],
            compiler_params=params(8),
            name="states_kept" if keep else "states_sent",
        )(ends, own, other, *operands, taps, bias)

    sent, compact = states(False, raw, other_raw, step_bias, rate_log)
    got = swap(sent, rows)
    kept, = states(True, compact)
    corner = jax.ShapeDtypeStruct((RIM, columns + 128), BF16)
    rim_sent, rim_kept = pl.pallas_call(
        functools.partial(rim_kernel, dims),
        out_shape=(corner, corner),
        in_specs=[VMEM] * 8,
        out_specs=(VMEM, VMEM),
        compiler_params=params(4),
        name="rim_terms",
    )(ends, own, other, rim, other_rim, compact, taps, bias)
    rim_got = swap(rim_sent, rows)
    plane, far, base = pl.pallas_call(
        functools.partial(plane_kernel, state), out_shape=(packed, piece, packed_wide), in_specs=[VMEM] * 4, out_specs=(VMEM,) * 3,
        compiler_params=params(4), name="plane_total",
    )(kept, rim_kept, got, rim_got)
    parts = []
    for back in range(1, reach + 1):
        for parity in range(2):
            pairs = [
                (GROUPS * p + q, GROUPS * (p + back) + q)
                for p in range(planes - back) if p // back % 2 == parity
                for q in range(GROUPS)
            ]
            payload = far if back == reach else plane
            parts.append(swap(payload, pairs) if pairs else parts[-1])

    a, b, c, own_state = pl.pallas_call(
        functools.partial(local_kernel, (heads, width, state, tok)),
        out_shape=(
            jax.ShapeDtypeStruct((tok, inner), F32),
            jax.ShapeDtypeStruct((tok, inner), F32),
            jax.ShapeDtypeStruct((GROUPS, tok, state), BF16),
            jax.ShapeDtypeStruct((state + 8, inner), BF16),
        ),
        in_specs=[VMEM] * 4 + [HBM] + [VMEM] * 6,
        out_specs=(VMEM,) * 4,
        scratch_shapes=[pltpu.VMEM((tok, inner), BF16), pltpu.SemaphoreType.DMA],
        compiler_params=params(16),
        name="local_block",
    )(ends, own, other, rim, hbm(gate_in), raw, step_bias, rate_log, taps, bias, skip_gain)
    prior = swap(own_state, cores)

    x0, mine = pl.pallas_call(
        functools.partial(arrive_kernel, reach, state), out_shape=(piece, piece), in_specs=[VMEM] * (1 + 2 * reach),
        out_specs=(VMEM, VMEM), compiler_params=params(4), name="arrive",
    )(base, *parts)
    x1 = swap(mine, rows)
    x2 = swap(x0, cores)
    x3 = swap(x1, cores)

    common = (a, b, c, prior, norm_gain)
    whole_out = jax.ShapeDtypeStruct((tok, inner), BF16)
    ready = [pltpu.VMEM((2, tok, columns), BF16), pltpu.SemaphoreType.DMA((2,))]
    out = pl.pallas_call(
        functools.partial(finish_near_kernel, width), out_shape=whole_out, in_specs=[VMEM] * 7, out_specs=HBM,
        scratch_shapes=ready, compiler_params=params(8), name="finish_near",
    )(*common, x0, x2)
    back_piece = pl.pallas_call(
        functools.partial(finish_back_kernel, width), out_shape=jax.ShapeDtypeStruct((tok, columns), BF16),
        in_specs=[VMEM] * 6, out_specs=VMEM, compiler_params=params(8), name="finish_back",
    )(*common, x1)
    return pl.pallas_call(
        functools.partial(finish_far_kernel, width), out_shape=whole_out, in_specs=[VMEM] * 7 + [HBM], out_specs=HBM,
        scratch_shapes=[pltpu.VMEM((tok, columns), BF16), pltpu.SemaphoreType.DMA((2,))],
        input_output_aliases={7: 0}, compiler_params=params(8), name="finish_far",
    )(*common, x3, back_piece, out)


def solution(mesh):
    split_rows = P(("groups", "seq"), None)
    return jax.shard_map(
        on_device,
        mesh=mesh,
        in_specs=(split_rows, split_rows, split_rows, P(), P(), P(), P(), P(), P(), P("groups")),
        out_specs=split_rows,
        check_vma=False,
    )
```

```python
import functools

import jax
import jax.numpy as jnp
from jax import lax
from jax.experimental import pallas as pl
from jax.experimental.pallas import tpu as pltpu
from jax.sharding import PartitionSpec as P

GROUPS = 4
PAIR = 2
RIM = 8
BLOCK = 256
EPSILON = 1e-05
F32 = jnp.float32
BF16 = jnp.bfloat16
VMEM = pl.BlockSpec(memory_space=pltpu.VMEM)
HBM = pl.BlockSpec(memory_space=pltpu.HBM)


def dot(a, b, dims=((1,), (0,))):
    return lax.dot_general(a, b, (dims, ((), ())), preferred_element_type=F32)


def silu(v):
    half = 0.5 * v
    return half + half * jnp.tanh(half)


def split(a, parts):
    out = []
    for _ in range(parts):
        top = a.astype(BF16)
        out.append(top)
        a = a - top.astype(F32)
    return out


def start_of(ends, position):
    start = jnp.zeros(position.shape, jnp.int32)
    for i in range(ends.shape[0]):
        end = ends[i : i + 1, : position.shape[1]]
        start = jnp.where(position >= end, end, start)
    return start


def start_at(ends, place):
    return start_of(ends, jnp.broadcast_to(place, (1, ends.shape[1])))


def log_sums(raw, bias, rate_log):
    v = raw.astype(F32) + bias
    step = jnp.maximum(v, 0.0) + jnp.log(1.0 + jnp.exp(-jnp.abs(v)))
    change = -jnp.exp(rate_log) * step
    down, across = (lax.broadcasted_iota(jnp.int32, (raw.shape[0],) * 2, k) for k in range(2))
    lower = jnp.where(across <= down, 1.0, 0.0).astype(BF16)
    sums = sum(dot(lower, part) for part in split(change, 3))
    return step, sums


def selector(heads, columns, width, first):
    start = (lax.broadcasted_iota(jnp.int32, (heads, 128), 0) - first) * width
    lane = lax.broadcasted_iota(jnp.int32, (heads, 128), 1)
    tiles = []
    for j in range(columns // 128):
        column = lane + j * 128
        tiles.append(jnp.where((column >= start) & (column < start + width), 1.0, 0.0))
    once = jnp.concatenate(tiles, axis=1).astype(BF16)
    return jnp.concatenate([once] * 3, axis=0)


def widen(compact, chosen):
    return dot(jnp.concatenate([p.astype(F32) for p in split(compact, 3)], axis=1).astype(BF16), chosen)


def shifts(starts, first, places, count):
    down = lax.broadcasted_iota(jnp.int32, places.shape, 0)
    inside = jnp.where(places + first >= starts[:, : places.shape[1]], 1.0, 0.0)
    back = down - places
    return jnp.concatenate([jnp.where(back == k, inside, 0.0) for k in range(count)], axis=0).astype(BF16)


def convolve(moves, rows, taps, bias):
    count = taps.shape[0]
    length = moves.shape[0] // count
    moved = dot(moves, rows)
    half = 0.5 * bias
    for back in range(count):
        half = half + (0.5 * taps[count - 1 - back : count - back]) * moved[back * length : (back + 1) * length]
    return (half + half * jnp.tanh(half)).astype(BF16)


def convolve_few(rows, reached, taps, bias):
    count = taps.shape[0]
    half = 0.5 * bias + (0.5 * taps[count - 1 :]) * rows[RIM:]
    for back in range(1, count):
        moved = pltpu.roll(rows, back, 0)[RIM:]
        half = half + (0.5 * taps[count - 1 - back : count - back]) * jnp.where(reached[back - 1], moved, 0.0)
    return (half + half * jnp.tanh(half)).astype(BF16)


def pick(first, a, b):
    return jnp.where(first, a, b)


def load_kernel(dims, lengths, rows, raw, step_bias, rate_log, taps, bias, out_rows, packed, out_raw, out_bias, out_rate, out_taps,
                out_conv, ends, lens, rim, sems):
    tok = rows.shape[0]
    inner, pair = dims
    moves = [
        (lengths, lens), (rows.at[tok - RIM :], rim), (raw, out_raw), (step_bias, out_bias), (rate_log, out_rate),
        (taps, out_taps), (bias, out_conv), (rows, out_rows),
    ]
    copies = [pltpu.make_async_copy(a, b, sems.at[k]) for k, (a, b) in enumerate(moves)]
    for copy in copies:
        copy.start()
    copies[0].wait()
    end = jnp.int32(0)
    for i in range(lengths.shape[0]):
        end = end + lens[i]
        ends[i : i + 1] = jnp.broadcast_to(end, (1, 128))
    copies[1].wait()
    segments = []
    for k in range(PAIR):
        starts = ((k * inner // PAIR, inner // PAIR), (inner + k * pair, pair), (inner + (PAIR + k) * pair, pair))
        segments.append(jnp.concatenate([rim[:, a : a + n].astype(F32) for a, n in starts], axis=1))
    down = lax.broadcasted_iota(jnp.int32, segments[0].shape, 0)
    mixed = jnp.where(down < 3, pltpu.roll(segments[0], 3, 0), pltpu.roll(segments[1], 6, 0))
    packed[...] = mixed.astype(BF16)
    for copy in copies[2:]:
        copy.wait()


def unpacked(packed, lanes, second):
    rows = packed[:, lanes].astype(F32)
    return pick(second, pltpu.roll(rows, 2, 0), pltpu.roll(rows, 5, 0))


def states_kernel(keep, dims, state, ends_ref, own, other, *rest):
    heads, width, inner, tok = dims
    if keep:
        compact, taps, bias, out, weighted = rest
    else:
        raw_own, raw_other, step_bias, rate_log, taps, bias, out, compact, weighted = rest
    index = lax.axis_index("seq")
    core, row = index % 2, (index // 2) % 2
    columns = inner // GROUPS
    wanted = row if keep else 1 - row
    group = PAIR * core + wanted
    at = pl.multiple_of(group * columns, columns)
    at_b = pl.multiple_of(inner + core * 128, 128)
    is_first = core == 0
    chip_first = (index - core) * tok
    ends = ends_ref[...]
    first_at = pick(is_first, 0, tok)
    column = lax.broadcasted_iota(jnp.int32, (2 * tok, 2 * tok), 1)
    places = jnp.where(column < tok, column + first_at, column - first_at)
    position = lax.broadcasted_iota(jnp.int32, (2 * tok, 128), 0) + chip_first
    moves = shifts(start_of(ends, position), chip_first, places, taps.shape[0])
    if not keep:
        prior = chip_first - 1
        start_a, start_b = (start_at(ends, chip_first + place)[:, :heads] for place in (tok - 1, 2 * tok - 1))
        one, two = (log_sums(raw[...], step_bias[...], rate_log[...]) for raw in (raw_own, raw_other))
        scales, lasts = [], []
        for part, start in enumerate((start_a, start_b)):
            step, sums = (pick(is_first == (part == 0), a, b) for a, b in zip(one, two))
            last = sums[tok - 1 :]
            here = position[part * tok : (part + 1) * tok, :heads] >= start
            scales.append(jnp.where(here, jnp.exp(last - sums) * step, 0.0))
            lasts.append(jnp.exp(last))
        pass_a = jnp.where(start_a <= prior, lasts[0], 0.0)
        pass_b = jnp.where(start_b <= prior + tok, lasts[1], 0.0)
        compact[:RIM] = jnp.zeros((RIM, heads), F32)
        compact[RIM:tok] = scales[0][RIM:]
        compact[tok : 2 * tok] = scales[1]
        which = lax.broadcasted_iota(jnp.int32, (8, heads), 0)
        compact[2 * tok : 2 * tok + 8] = jnp.where(which == 0, pass_b, jnp.where(which == 1, pass_a * pass_b, 0.0))
        compact[2 * tok + 8 :] = scales[0][:RIM] * pass_b
    scale = widen(compact[: 2 * tok + 8], selector(heads, columns, width, group * (heads // GROUPS)))


    def mixed(lanes_at, size):
        rows = jnp.concatenate([own[:, lanes_at], other[:, lanes_at]], axis=0)
        return convolve(moves, rows, taps[:, lanes_at], bias[lanes_at].reshape(1, size)).astype(F32)

    b_pair = mixed(pl.ds(at_b, 128), 128)
    half = b_pair.shape[1] // 2
    b_rows = pick(wanted == 0, b_pair[:, :half], b_pair[:, half:]).astype(BF16)
    for j in range(columns // BLOCK):
        lanes = slice(j * BLOCK, (j + 1) * BLOCK)
        x = mixed(pl.ds(pl.multiple_of(at + j * BLOCK, BLOCK), BLOCK), BLOCK)
        weighted[:, lanes] = (x * scale[: 2 * tok, lanes]).astype(BF16)
    state_a = dot(b_rows[:tok], weighted[:tok], ((0,), (0,)))
    state_b = dot(b_rows[tok:], weighted[tok:], ((0,), (0,)))
    passes = scale[2 * tok + 1 : 2 * tok + 2]
    total = scale[2 * tok : 2 * tok + 1] * state_a + state_b
    if keep:
        out[:state] = total
        out[state:] = jnp.broadcast_to(passes, (8, columns))
    else:
        pack(out, total, passes)


def rim_kernel(dims, ends, own, other, rim_own, rim_other, compact, taps, bias, out_sent, out_kept):
    heads, width, inner, tok = dims
    index = lax.axis_index("seq")
    core, row = index % 2, (index // 2) % 2
    columns = inner // GROUPS
    at = pl.multiple_of(PAIR * core * columns, PAIR * columns)
    at_b = pl.multiple_of(inner + core * 128, 128)
    is_first = core == 0
    chip_first = (index - core) * tok
    position = lax.broadcasted_iota(jnp.int32, (RIM, 128), 0) + chip_first
    starts = start_of(ends[...], position)
    reached = [position - back >= starts for back in range(1, taps.shape[0])]
    scale = widen(compact[2 * tok + 8 :], selector(heads, PAIR * columns, width, core * (heads // PAIR)))

    def mixed(lanes_at, lanes):
        rim = pick(is_first, unpacked(rim_own, lanes, False), unpacked(rim_other, lanes, True))
        top = pick(is_first, own[:RIM, lanes_at].astype(F32), other[:RIM, lanes_at].astype(F32))
        rows = jnp.concatenate([rim, top], axis=0)
        return convolve_few(rows, reached, taps[:, lanes_at], bias[lanes_at].reshape(1, 128)).astype(F32)

    b_pair = mixed(pl.ds(at_b, 128), slice(PAIR * columns, PAIR * columns + 128))
    half = b_pair.shape[1] // 2
    upper = row == 1
    for out, which in ((out_sent, row == 0), (out_kept, upper)):
        b_rows = pick(which, b_pair[:, half:], b_pair[:, :half])
        out[:, columns:] = jnp.concatenate([b_rows, jnp.zeros_like(b_rows)], axis=1).astype(BF16)
    for j in range(columns // 128):
        lanes = slice(j * 128, (j + 1) * 128)
        behind = slice(columns + j * 128, columns + (j + 1) * 128)
        low = mixed(pl.ds(pl.multiple_of(at + j * 128, 128), 128), lanes) * scale[:, lanes]
        high = mixed(pl.ds(pl.multiple_of(at + columns + j * 128, 128), 128), behind) * scale[:, behind]
        out_sent[:, lanes] = pick(upper, low, high).astype(BF16)
        out_kept[:, lanes] = pick(upper, high, low).astype(BF16)


def late(rows, state, columns):
    return dot(rows[:, columns : columns + state], rows[:, :columns], ((0,), (0,)))


def two_rows(passes, shape):
    top = passes.astype(BF16).astype(F32)
    which = lax.broadcasted_iota(jnp.int32, shape, 0)
    both = jnp.where(which == 0, top, jnp.where(which == 1, passes - top, 0.0))
    return both.astype(BF16)


def pack(out, state, passes):
    rows, tiles = state.shape[0], state.shape[1] // 128
    spread = [slice(k * 128, (k + 1) * 128) for k in range(tiles)]
    for k, lanes in enumerate(spread):
        out[k * rows : (k + 1) * rows] = state[:, lanes].astype(BF16)
    top, rest = split(jnp.concatenate([passes[:, lanes] for lanes in spread], axis=0), 2)
    out[tiles * rows : tiles * rows + tiles] = top
    out[tiles * rows + tiles :] = rest


def unpack(payload, rows, columns):
    tiles = columns // 128
    state = jnp.concatenate([payload[k * rows : (k + 1) * rows].astype(F32) for k in range(tiles)], axis=1)
    first = tiles * rows
    wide = payload[first : first + tiles].astype(F32) + payload[first + tiles :].astype(F32)
    return state, jnp.concatenate([wide[k : k + 1] for k in range(tiles)], axis=1)


def plane_kernel(state, own, own_rim, got, got_rim, out, far, base):
    upper = (lax.axis_index("seq") // 2) % 2 == 1
    mine = own[:state] + late(own_rim[...], state, own.shape[1])
    theirs, their_pass = unpack(got[...], state, own.shape[1])
    theirs = theirs + late(got_rim[...], state, own.shape[1])
    my_pass = own[state : state + 1]
    first, second = pick(upper, theirs, mine), pick(upper, mine, theirs)
    first_pass, later_pass = pick(upper, their_pass, my_pass), pick(upper, my_pass, their_pass)
    total = (later_pass * first + second).astype(BF16)
    far[...] = total
    pack(out, total.astype(F32), my_pass * their_pass)
    base[:state] = first
    base[state:] = jnp.broadcast_to(first_pass, (8, own.shape[1]))


def arrive_kernel(reach, rows, base, *rest):
    parts, (out_own, out_sent) = rest[:-2], rest[-2:]
    index = lax.axis_index("seq")
    plane = index // GROUPS
    upper = (index // 2) % 2 == 1
    for back in range(reach, 0, -1):
        even, odd = parts[2 * (back - 1) : 2 * back]
        source = plane - back
        is_even = (source + 2 * back) // back % 2 == 0
        there = source >= 0
        arrived = jnp.where(there, pick(is_even, even[...].astype(F32), odd[...].astype(F32)), 0.0)
        if back == reach:
            state = arrived
        else:
            fresh, passes = unpack(arrived, rows, base.shape[1])
            state = fresh + passes * state
    later = base[rows : rows + 1] * state + base[:rows]
    out_own[...] = pick(upper, later, state).astype(BF16)
    out_sent[...] = pick(upper, state, later).astype(BF16)


def local_kernel(dims, ends_ref, own, other, rim, gate_hbm, raw, step_bias, rate_log, taps, bias, skip,
                 a_out, b_out, c_out, s_out, gate, sem):
    heads, width, state, tok = dims
    copy = pltpu.make_async_copy(gate_hbm, gate, sem)
    copy.start()
    index = lax.axis_index("seq")
    is_first = index % 2 == 0
    first = index * tok
    inner, per = gate.shape[1], heads // GROUPS
    columns = inner // GROUPS
    ends = ends_ref[...]
    position = lax.broadcasted_iota(jnp.int32, (tok, 128), 0) + first
    starts = start_of(ends, position)
    final = start_at(ends, first + tok - 1)
    column = lax.broadcasted_iota(jnp.int32, (tok, tok + 2 * RIM), 1)
    places = jnp.where(column < tok, column, jnp.where(column < tok + RIM, column - tok - RIM, tok))
    moves = shifts(starts, first, places, taps.shape[0])

    def rim_rows(lanes):
        if lanes.start < inner:
            second, at = divmod(lanes.start, inner // PAIR)
            return unpacked(rim, slice(at, at + BLOCK), second == 1)
        at = inner // PAIR + (lanes.start - inner) // PAIR
        halves = [unpacked(rim, slice(at, at + BLOCK // PAIR), k == 1) for k in range(PAIR)]
        return jnp.concatenate(halves, axis=1)

    def mixed(lanes):
        top = pick(is_first, rim_rows(lanes), other[tok - RIM :, lanes].astype(F32))
        extra = jnp.concatenate([top, jnp.zeros_like(top)], axis=0).astype(BF16)
        rows = jnp.concatenate([own[:, lanes], extra], axis=0)
        return convolve(moves, rows, taps[:, lanes], bias[lanes].reshape(1, lanes.stop - lanes.start)).astype(F32)

    b_all, c_all = [], []
    for j in range(2 * GROUPS * state // BLOCK):
        pieces = mixed(slice(inner + j * BLOCK, inner + (j + 1) * BLOCK))
        for k in range(BLOCK // state):
            (b_all if len(b_all) < GROUPS else c_all).append(pieces[:, k * state : (k + 1) * state].astype(BF16))
    step, sums = log_sums(raw[...], step_bias[...], rate_log[...])
    ending_decay = jnp.exp(sums[tok - 1 :])
    passed = jnp.where(final[:, :heads] < first, ending_decay, 0.0)
    rest = jnp.concatenate([ending_decay, passed, skip[...], jnp.zeros((5, heads), F32)], axis=0)
    whole = jnp.concatenate([jnp.exp(sums), jnp.exp(-sums) * step, rest], axis=0)
    chosen = selector(per, columns, width, 0)
    down, across = (lax.broadcasted_iota(jnp.int32, (tok, tok), k) for k in range(2))
    causal = (down >= across) & (across + first >= starts[:, :tok])
    here = position[:, :state] >= final[:, :state]
    entered = jnp.concatenate([starts] * (BLOCK // 128), axis=1) < first
    copy.wait()
    for g in range(GROUPS):
        wide = widen(whole[:, g * per : (g + 1) * per], chosen)
        b_rows, c_rows = b_all[g], c_all[g]
        c_out[g] = c_rows
        mask = jnp.where(causal, dot(c_rows, b_rows, ((1,), (1,))), 0.0)
        m_top, m_rest = split(mask, 2)
        lhs = jnp.concatenate([m_top.astype(F32), m_rest.astype(F32)], axis=1).astype(BF16)
        ending = jnp.where(here, b_rows.astype(F32), 0.0).astype(BF16)
        for j in range(columns // BLOCK):
            part = slice(j * BLOCK, (j + 1) * BLOCK)
            lanes = slice(g * columns + j * BLOCK, g * columns + (j + 1) * BLOCK)
            inward, outward = wide[:tok, part], wide[tok : 2 * tok, part]
            end_decay, gain = wide[2 * tok : 2 * tok + 1, part], wide[2 * tok + 2 : 2 * tok + 3, part]
            x = mixed(lanes)
            s_top, s_rest = split(x * outward, 2)
            within = dot(lhs, jnp.concatenate([s_top, s_top], axis=0)) + dot(m_top, s_rest)
            local = dot(ending, s_top, ((0,), (0,))) + dot(ending, s_rest, ((0,), (0,)))
            opened = silu(gate[:, lanes].astype(F32))
            a_out[:, lanes] = (inward * within + gain * x) * opened
            b_out[:, lanes] = jnp.where(entered, inward * opened, 0.0)
            s_out[:state, lanes] = (end_decay * local).astype(BF16)
        s_out[state:, g * columns : (g + 1) * columns] = two_rows(wide[2 * tok + 1 : 2 * tok + 2], (8, columns))


def place_of(far_core, far_row):
    index = lax.axis_index("seq")
    core, row = index % 2, (index // 2) % 2
    return PAIR * (1 - core if far_core else core) + (1 - row if far_row else row)


def finish_piece(width, group, arrived, a_ref, b_ref, c_ref, prior, gain, put):
    second = lax.axis_index("seq") % 2 == 1
    state_rows, columns = arrived.shape
    block = BLOCK
    down, across = (lax.broadcasted_iota(jnp.int32, (block, block), k) for k in range(2))
    low = across - lax.rem(across, width)
    means = jnp.where((down >= low) & (down < low + width), 1.0 / width, 0.0).astype(BF16)
    c_rows = c_ref[group]
    for j in range(columns // block):
        lanes = slice(j * block, (j + 1) * block)
        at = pl.ds(pl.multiple_of(group * columns + j * block, block), block)
        state = arrived[:, lanes].astype(F32)
        before = prior[:, at].astype(F32)
        stepped = (before[state_rows : state_rows + 1] + before[state_rows + 1 : state_rows + 2]) * state + before[:state_rows]
        state = pick(second, stepped, state).astype(BF16)
        gated = a_ref[:, at] + b_ref[:, at] * dot(c_rows, state)
        mean = dot((gated * gated).astype(BF16), means)
        put(lanes, (gated * lax.rsqrt(mean + EPSILON) * gain[:, at]).astype(BF16))


def finish_near_kernel(width, a, b, c, prior, gain, x0, x2, out, ready, sems):
    columns, copies = x0.shape[1], []
    for k, arrived in enumerate((x0, x2)):
        group = place_of(k == 1, False)

        def put(lanes, value, k=k):
            ready[k, :, lanes] = value

        finish_piece(width, group, arrived, a, b, c, prior, gain, put)
        target = out.at[:, pl.ds(pl.multiple_of(group * columns, columns), columns)]
        copies.append(pltpu.make_async_copy(ready.at[k], target, sems.at[k]))
        copies[-1].start()
    for copy in copies:
        copy.wait()


def finish_back_kernel(width, a, b, c, prior, gain, x1, out):
    def put(lanes, value):
        out[:, lanes] = value

    finish_piece(width, place_of(False, True), x1, a, b, c, prior, gain, put)


def finish_far_kernel(width, a, b, c, prior, gain, x3, piece, begun, out, ready, sems):
    columns = x3.shape[1]

    def target(group):
        return out.at[:, pl.ds(pl.multiple_of(group * columns, columns), columns)]

    early = pltpu.make_async_copy(piece, target(place_of(False, True)), sems.at[0])
    early.start()

    def put(lanes, value):
        ready[:, lanes] = value

    group = place_of(True, True)
    finish_piece(width, group, x3, a, b, c, prior, gain, put)
    copy = pltpu.make_async_copy(ready, target(group), sems.at[1])
    copy.start()
    early.wait()
    copy.wait()


def swap(block, pairs):
    return lax.ppermute(block, "seq", [*pairs, *((b, a) for a, b in pairs)])


def on_device(mixer_in, gate_in, step_raw, step_bias, rate_log, conv_weight, conv_bias, skip_gain, norm_gain, doc_lengths):
    tok, channels = mixer_in.shape
    heads, inner = rate_log.shape[0], gate_in.shape[1]
    width = inner // heads
    state = (channels - inner) // (2 * GROUPS)
    devices = lax.axis_size("seq")
    planes = devices // GROUPS
    columns = inner // GROUPS
    taps_n = conv_weight.shape[0]
    longest = devices * tok // 2
    reach = -(-(longest - 1) // (GROUPS * tok))
    row = lambda a: a.reshape(1, -1)
    step_bias, rate_log, skip_gain, norm_gain = map(row, (step_bias, rate_log, skip_gain, norm_gain))
    cores = [(i, i + 1) for i in range(0, devices, 2)]
    rows = [(i, i + 2) for i in range(0, devices, 4) for i in (i, i + 1)]
    chips = [(i, i + 1) for i in range(1, devices - 1, 2)]

    def hbm(block):
        return pltpu.with_memory_space_constraint(block, pltpu.HBM)

    other = swap(mixer_in, cores)
    other_raw = swap(step_raw, cores)
    own, rim, raw, step_bias, rate_log, taps, bias, ends = pl.pallas_call(
        functools.partial(load_kernel, (inner, PAIR * state)),
        out_shape=(
            jax.ShapeDtypeStruct((tok, channels), BF16), jax.ShapeDtypeStruct((RIM, channels // PAIR), BF16),
            jax.ShapeDtypeStruct((tok, heads), BF16), jax.ShapeDtypeStruct((1, heads), F32),
            jax.ShapeDtypeStruct((1, heads), F32), jax.ShapeDtypeStruct((taps_n, channels), F32),
            jax.ShapeDtypeStruct((channels,), F32), jax.ShapeDtypeStruct((doc_lengths.shape[0], 128), jnp.int32),
        ),
        in_specs=[HBM] * 7,
        out_specs=(VMEM,) * 8,
        scratch_shapes=[pltpu.SMEM(doc_lengths.shape, jnp.int32), pltpu.VMEM((RIM, channels), BF16), pltpu.SemaphoreType.DMA((8,))],
        compiler_params=pltpu.CompilerParams(vmem_limit_bytes=4 << 20),
        name="load",
    )(*map(hbm, (doc_lengths, mixer_in, step_raw, step_bias, rate_log, conv_weight, conv_bias)))
    rim = swap(rim, chips)
    other_rim = swap(rim, cores)

    def params(mib):
        return pltpu.CompilerParams(vmem_limit_bytes=mib << 20)

    packed = jax.ShapeDtypeStruct(((state + 2) * (columns // 128), 128), BF16)
    packed_wide = jax.ShapeDtypeStruct((state + 8, columns), F32)
    piece = jax.ShapeDtypeStruct((state, columns), BF16)
    dims = (heads, width, inner, tok)

    def states(keep, *operands):
        compact = () if keep else (jax.ShapeDtypeStruct((2 * tok + 16, heads), F32),)
        return pl.pallas_call(
            functools.partial(states_kernel, keep, dims, state),
            out_shape=(packed_wide if keep else packed, *compact),
            in_specs=[VMEM] * (3 + len(operands) + 2),
            out_specs=(VMEM,) * (1 + len(compact)),
            scratch_shapes=[pltpu.VMEM((2 * tok, columns), BF16)],
            compiler_params=params(8),
            name="states_kept" if keep else "states_sent",
        )(ends, own, other, *operands, taps, bias)

    sent, compact = states(False, raw, other_raw, step_bias, rate_log)
    got = swap(sent, rows)
    kept, = states(True, compact)
    corner = jax.ShapeDtypeStruct((RIM, columns + 128), BF16)
    rim_sent, rim_kept = pl.pallas_call(
        functools.partial(rim_kernel, dims),
        out_shape=(corner, corner),
        in_specs=[VMEM] * 8,
        out_specs=(VMEM, VMEM),
        compiler_params=params(4),
        name="rim_terms",
    )(ends, own, other, rim, other_rim, compact, taps, bias)
    rim_got = swap(rim_sent, rows)
    plane, far, base = pl.pallas_call(
        functools.partial(plane_kernel, state), out_shape=(packed, piece, packed_wide), in_specs=[VMEM] * 4, out_specs=(VMEM,) * 3,
        compiler_params=params(4), name="plane_total",
    )(kept, rim_kept, got, rim_got)
    parts = []
    for back in range(1, reach + 1):
        for parity in range(2):
            pairs = [
                (GROUPS * p + q, GROUPS * (p + back) + q)
                for p in range(planes - back) if p // back % 2 == parity
                for q in range(GROUPS)
            ]
            payload = far if back == reach else plane
            parts.append(swap(payload, pairs) if pairs else parts[-1])

    a, b, c, own_state = pl.pallas_call(
        functools.partial(local_kernel, (heads, width, state, tok)),
        out_shape=(
            jax.ShapeDtypeStruct((tok, inner), F32),
            jax.ShapeDtypeStruct((tok, inner), F32),
            jax.ShapeDtypeStruct((GROUPS, tok, state), BF16),
            jax.ShapeDtypeStruct((state + 8, inner), BF16),
        ),
        in_specs=[VMEM] * 4 + [HBM] + [VMEM] * 6,
        out_specs=(VMEM,) * 4,
        scratch_shapes=[pltpu.VMEM((tok, inner), BF16), pltpu.SemaphoreType.DMA],
        compiler_params=params(16),
        name="local_block",
    )(ends, own, other, rim, hbm(gate_in), raw, step_bias, rate_log, taps, bias, skip_gain)
    prior = swap(own_state, cores)

    x0, mine = pl.pallas_call(
        functools.partial(arrive_kernel, reach, state), out_shape=(piece, piece), in_specs=[VMEM] * (1 + 2 * reach),
        out_specs=(VMEM, VMEM), compiler_params=params(4), name="arrive",
    )(base, *parts)
    x1 = swap(mine, rows)
    x2 = swap(x0, cores)
    x3 = swap(x1, cores)

    common = (a, b, c, prior, norm_gain)
    whole_out = jax.ShapeDtypeStruct((tok, inner), BF16)
    ready = [pltpu.VMEM((2, tok, columns), BF16), pltpu.SemaphoreType.DMA((2,))]
    out = pl.pallas_call(
        functools.partial(finish_near_kernel, width), out_shape=whole_out, in_specs=[VMEM] * 7, out_specs=HBM,
        scratch_shapes=ready, compiler_params=params(8), name="finish_near",
    )(*common, x0, x2)
    back_piece = pl.pallas_call(
        functools.partial(finish_back_kernel, width), out_shape=jax.ShapeDtypeStruct((tok, columns), BF16),
        in_specs=[VMEM] * 6, out_specs=VMEM, compiler_params=params(8), name="finish_back",
    )(*common, x1)
    return pl.pallas_call(
        functools.partial(finish_far_kernel, width), out_shape=whole_out, in_specs=[VMEM] * 7 + [HBM], out_specs=HBM,
        scratch_shapes=[pltpu.VMEM((tok, columns), BF16), pltpu.SemaphoreType.DMA((2,))],
        input_output_aliases={7: 0}, compiler_params=params(8), name="finish_far",
    )(*common, x3, back_piece, out)


def solution(mesh):
    split_rows = P(("groups", "seq"), None)
    return jax.shard_map(
        on_device,
        mesh=mesh,
        in_specs=(split_rows, split_rows, split_rows, P(), P(), P(), P(), P(), P(), P("groups")),
        out_specs=split_rows,
        check_vma=False,
    )
```

```python
import functools

import jax
import jax.numpy as jnp
from jax import lax
from jax.experimental import pallas as pl
from jax.experimental.pallas import tpu as pltpu
from jax.sharding import PartitionSpec as P

GROUPS = 4
PAIR = 2
RIM = 8
BLOCK = 256
EPSILON = 1e-05
F32 = jnp.float32
BF16 = jnp.bfloat16
VMEM = pl.BlockSpec(memory_space=pltpu.VMEM)
HBM = pl.BlockSpec(memory_space=pltpu.HBM)


def dot(a, b, dims=((1,), (0,))):
    return lax.dot_general(a, b, (dims, ((), ())), preferred_element_type=F32)


def silu(v):
    half = 0.5 * v
    return half + half * jnp.tanh(half)


def split(a, parts):
    out = []
    for _ in range(parts):
        top = a.astype(BF16)
        out.append(top)
        a = a - top.astype(F32)
    return out


def start_of(ends, position):
    start = jnp.zeros(position.shape, jnp.int32)
    for i in range(ends.shape[0]):
        end = ends[i : i + 1, : position.shape[1]]
        start = jnp.where(position >= end, end, start)
    return start


def start_at(ends, place):
    return start_of(ends, jnp.broadcast_to(place, (1, ends.shape[1])))


def log_sums(raw, bias, rate_log):
    v = raw.astype(F32) + bias
    step = jnp.maximum(v, 0.0) + jnp.log(1.0 + jnp.exp(-jnp.abs(v)))
    change = -jnp.exp(rate_log) * step
    down, across = (lax.broadcasted_iota(jnp.int32, (raw.shape[0],) * 2, k) for k in range(2))
    lower = jnp.where(across <= down, 1.0, 0.0).astype(BF16)
    sums = sum(dot(lower, part) for part in split(change, 3))
    return step, sums


def selector(heads, columns, width, first):
    start = (lax.broadcasted_iota(jnp.int32, (heads, 128), 0) - first) * width
    lane = lax.broadcasted_iota(jnp.int32, (heads, 128), 1)
    tiles = []
    for j in range(columns // 128):
        column = lane + j * 128
        tiles.append(jnp.where((column >= start) & (column < start + width), 1.0, 0.0))
    once = jnp.concatenate(tiles, axis=1).astype(BF16)
    return jnp.concatenate([once] * 2, axis=0)


def widen(compact, chosen):
    return dot(jnp.concatenate([p.astype(F32) for p in split(compact, 2)], axis=1).astype(BF16), chosen)


def shifts(starts, first, places, count):
    down = lax.broadcasted_iota(jnp.int32, places.shape, 0)
    inside = jnp.where(places + first >= starts[:, : places.shape[1]], 1.0, 0.0)
    back = down - places
    return jnp.concatenate([jnp.where(back == k, inside, 0.0) for k in range(count)], axis=0).astype(BF16)


def convolve(moves, rows, taps, bias):
    count = taps.shape[0]
    length = moves.shape[0] // count
    moved = dot(moves, rows)
    half = 0.5 * bias
    for back in range(count):
        half = half + (0.5 * taps[count - 1 - back : count - back]) * moved[back * length : (back + 1) * length]
    return (half + half * jnp.tanh(half)).astype(BF16)


def convolve_few(rows, reached, taps, bias):
    count = taps.shape[0]
    half = 0.5 * bias + (0.5 * taps[count - 1 :]) * rows[RIM:]
    for back in range(1, count):
        moved = pltpu.roll(rows, back, 0)[RIM:]
        half = half + (0.5 * taps[count - 1 - back : count - back]) * jnp.where(reached[back - 1], moved, 0.0)
    return (half + half * jnp.tanh(half)).astype(BF16)


def pick(first, a, b):
    return jnp.where(first, a, b)


def load_kernel(dims, lengths, rows, raw, step_bias, rate_log, taps, bias, out_rows, packed, out_raw, out_bias, out_rate, out_taps,
                out_conv, ends, lens, rim, sems):
    tok = rows.shape[0]
    inner, pair = dims
    moves = [
        (lengths, lens), (rows.at[tok - RIM :], rim), (raw, out_raw), (step_bias, out_bias), (rate_log, out_rate),
        (taps, out_taps), (bias, out_conv),
    ]
    core = lax.axis_index("seq") % 2
    for at, size in ((core * (inner // PAIR), inner // PAIR), (inner + core * pair, pair)):
        lanes = pl.ds(pl.multiple_of(at, size), size)
        moves.append((rows.at[:, lanes], out_rows.at[:, lanes]))
    copies = [pltpu.make_async_copy(a, b, sems.at[k]) for k, (a, b) in enumerate(moves)]
    for copy in copies:
        copy.start()
    copies[0].wait()
    end = jnp.int32(0)
    for i in range(lengths.shape[0]):
        end = end + lens[i]
        ends[i : i + 1] = jnp.broadcast_to(end, (1, 128))
    copies[1].wait()
    segments = []
    for k in range(PAIR):
        starts = ((k * inner // PAIR, inner // PAIR), (inner + k * pair, pair), (inner + (PAIR + k) * pair, pair))
        segments.append(jnp.concatenate([rim[:, a : a + n].astype(F32) for a, n in starts], axis=1))
    down = lax.broadcasted_iota(jnp.int32, segments[0].shape, 0)
    mixed = jnp.where(down < 3, pltpu.roll(segments[0], 3, 0), pltpu.roll(segments[1], 6, 0))
    packed[...] = mixed.astype(BF16)
    for copy in copies[2:]:
        copy.wait()


def unpacked(packed, lanes, second):
    rows = packed[:, lanes].astype(F32)
    return pick(second, pltpu.roll(rows, 2, 0), pltpu.roll(rows, 5, 0))


def states_kernel(keep, dims, state, ends_ref, own, other, *rest):
    heads, width, inner, tok = dims
    if keep:
        compact, taps, bias, out, weighted = rest
    else:
        raw_own, raw_other, step_bias, rate_log, taps, bias, out, compact, weighted = rest
    index = lax.axis_index("seq")
    core, row = index % 2, (index // 2) % 2
    columns = inner // GROUPS
    wanted = row if keep else 1 - row
    group = PAIR * core + wanted
    at = pl.multiple_of(group * columns, columns)
    at_b = pl.multiple_of(inner + core * 128, 128)
    is_first = core == 0
    chip_first = (index - core) * tok
    ends = ends_ref[...]
    first_at = pick(is_first, 0, tok)
    column = lax.broadcasted_iota(jnp.int32, (2 * tok, 2 * tok), 1)
    places = jnp.where(column < tok, column + first_at, column - first_at)
    position = lax.broadcasted_iota(jnp.int32, (2 * tok, 128), 0) + chip_first
    moves = shifts(start_of(ends, position), chip_first, places, taps.shape[0])
    if not keep:
        prior = chip_first - 1
        start_a, start_b = (start_at(ends, chip_first + place)[:, :heads] for place in (tok - 1, 2 * tok - 1))
        one, two = (log_sums(raw[...], step_bias[...], rate_log[...]) for raw in (raw_own, raw_other))
        scales, lasts = [], []
        for part, start in enumerate((start_a, start_b)):
            step, sums = (pick(is_first == (part == 0), a, b) for a, b in zip(one, two))
            last = sums[tok - 1 :]
            here = position[part * tok : (part + 1) * tok, :heads] >= start
            scales.append(jnp.where(here, jnp.exp(last - sums) * step, 0.0))
            lasts.append(jnp.exp(last))
        pass_a = jnp.where(start_a <= prior, lasts[0], 0.0)
        pass_b = jnp.where(start_b <= prior + tok, lasts[1], 0.0)
        compact[:RIM] = jnp.zeros((RIM, heads), F32)
        compact[RIM:tok] = scales[0][RIM:]
        compact[tok : 2 * tok] = scales[1]
        which = lax.broadcasted_iota(jnp.int32, (8, heads), 0)
        compact[2 * tok : 2 * tok + 8] = jnp.where(which == 0, pass_b, jnp.where(which == 1, pass_a * pass_b, 0.0))
        compact[2 * tok + 8 :] = scales[0][:RIM] * pass_b
    scale = widen(compact[: 2 * tok + 8], selector(heads, columns, width, group * (heads // GROUPS)))


    def mixed(lanes_at, size):
        rows = jnp.concatenate([own[:, lanes_at], other[:, lanes_at]], axis=0)
        return convolve(moves, rows, taps[:, lanes_at], bias[lanes_at].reshape(1, size)).astype(F32)

    b_pair = mixed(pl.ds(at_b, 128), 128)
    half = b_pair.shape[1] // 2
    b_rows = pick(wanted == 0, b_pair[:, :half], b_pair[:, half:]).astype(BF16)
    for j in range(columns // BLOCK):
        lanes = slice(j * BLOCK, (j + 1) * BLOCK)
        x = mixed(pl.ds(pl.multiple_of(at + j * BLOCK, BLOCK), BLOCK), BLOCK)
        weighted[:, lanes] = (x * scale[: 2 * tok, lanes]).astype(BF16)
    state_a = dot(b_rows[:tok], weighted[:tok], ((0,), (0,)))
    state_b = dot(b_rows[tok:], weighted[tok:], ((0,), (0,)))
    passes = scale[2 * tok + 1 : 2 * tok + 2]
    total = scale[2 * tok : 2 * tok + 1] * state_a + state_b
    if keep:
        out[:state] = total
        out[state:] = jnp.broadcast_to(passes, (8, columns))
    else:
        pack(out, total, passes)


def rim_kernel(dims, ends, own, other, rim_own, rim_other, compact, taps, bias, out_sent, out_kept):
    heads, width, inner, tok = dims
    index = lax.axis_index("seq")
    core, row = index % 2, (index // 2) % 2
    columns = inner // GROUPS
    at = pl.multiple_of(PAIR * core * columns, PAIR * columns)
    at_b = pl.multiple_of(inner + core * 128, 128)
    is_first = core == 0
    chip_first = (index - core) * tok
    position = lax.broadcasted_iota(jnp.int32, (RIM, 128), 0) + chip_first
    starts = start_of(ends[...], position)
    reached = [position - back >= starts for back in range(1, taps.shape[0])]
    scale = widen(compact[2 * tok + 8 :], selector(heads, PAIR * columns, width, core * (heads // PAIR)))

    def mixed(lanes_at, lanes):
        rim = pick(is_first, unpacked(rim_own, lanes, False), unpacked(rim_other, lanes, True))
        top = pick(is_first, own[:RIM, lanes_at].astype(F32), other[:RIM, lanes_at].astype(F32))
        rows = jnp.concatenate([rim, top], axis=0)
        return convolve_few(rows, reached, taps[:, lanes_at], bias[lanes_at].reshape(1, 128)).astype(F32)

    b_pair = mixed(pl.ds(at_b, 128), slice(PAIR * columns, PAIR * columns + 128))
    half = b_pair.shape[1] // 2
    upper = row == 1
    for out, which in ((out_sent, row == 0), (out_kept, upper)):
        b_rows = pick(which, b_pair[:, half:], b_pair[:, :half])
        out[:, columns:] = jnp.concatenate([b_rows, jnp.zeros_like(b_rows)], axis=1).astype(BF16)
    for j in range(columns // 128):
        lanes = slice(j * 128, (j + 1) * 128)
        behind = slice(columns + j * 128, columns + (j + 1) * 128)
        low = mixed(pl.ds(pl.multiple_of(at + j * 128, 128), 128), lanes) * scale[:, lanes]
        high = mixed(pl.ds(pl.multiple_of(at + columns + j * 128, 128), 128), behind) * scale[:, behind]
        out_sent[:, lanes] = pick(upper, low, high).astype(BF16)
        out_kept[:, lanes] = pick(upper, high, low).astype(BF16)


def late(rows, state, columns):
    return dot(rows[:, columns : columns + state], rows[:, :columns], ((0,), (0,)))


def two_rows(passes, shape):
    top = passes.astype(BF16).astype(F32)
    which = lax.broadcasted_iota(jnp.int32, shape, 0)
    both = jnp.where(which == 0, top, jnp.where(which == 1, passes - top, 0.0))
    return both.astype(BF16)


def pack(out, state, passes):
    rows, tiles = state.shape[0], state.shape[1] // 128
    spread = [slice(k * 128, (k + 1) * 128) for k in range(tiles)]
    for k, lanes in enumerate(spread):
        out[k * rows : (k + 1) * rows] = state[:, lanes].astype(BF16)
    top, rest = split(jnp.concatenate([passes[:, lanes] for lanes in spread], axis=0), 2)
    out[tiles * rows : tiles * rows + tiles] = top
    out[tiles * rows + tiles :] = rest


def unpack(payload, rows, columns):
    tiles = columns // 128
    state = jnp.concatenate([payload[k * rows : (k + 1) * rows].astype(F32) for k in range(tiles)], axis=1)
    first = tiles * rows
    wide = payload[first : first + tiles].astype(F32) + payload[first + tiles :].astype(F32)
    return state, jnp.concatenate([wide[k : k + 1] for k in range(tiles)], axis=1)


def plane_kernel(state, own, own_rim, got, got_rim, out, far, base):
    upper = (lax.axis_index("seq") // 2) % 2 == 1
    mine = own[:state] + late(own_rim[...], state, own.shape[1])
    theirs, their_pass = unpack(got[...], state, own.shape[1])
    theirs = theirs + late(got_rim[...], state, own.shape[1])
    my_pass = own[state : state + 1]
    first, second = pick(upper, theirs, mine), pick(upper, mine, theirs)
    first_pass, later_pass = pick(upper, their_pass, my_pass), pick(upper, my_pass, their_pass)
    total = (later_pass * first + second).astype(BF16)
    far[...] = total
    pack(out, total.astype(F32), my_pass * their_pass)
    base[:state] = first
    base[state:] = jnp.broadcast_to(first_pass, (8, own.shape[1]))


def arrive_kernel(reach, rows, base, *rest):
    parts, (out_own, out_sent) = rest[:-2], rest[-2:]
    index = lax.axis_index("seq")
    plane = index // GROUPS
    upper = (index // 2) % 2 == 1
    for back in range(reach, 0, -1):
        even, odd = parts[2 * (back - 1) : 2 * back]
        source = plane - back
        is_even = (source + 2 * back) // back % 2 == 0
        there = source >= 0
        arrived = jnp.where(there, pick(is_even, even[...].astype(F32), odd[...].astype(F32)), 0.0)
        if back == reach:
            state = arrived
        else:
            fresh, passes = unpack(arrived, rows, base.shape[1])
            state = fresh + passes * state
    later = base[rows : rows + 1] * state + base[:rows]
    out_own[...] = pick(upper, later, state).astype(BF16)
    out_sent[...] = pick(upper, state, later).astype(BF16)


def local_kernel(dims, ends_ref, own_hbm, other, rim, gate_hbm, raw, step_bias, rate_log, taps, bias, skip,
                 a_out, b_out, c_out, s_out, gate, own, sems):
    heads, width, state, tok = dims
    copies = [pltpu.make_async_copy(own_hbm, own, sems.at[0]), pltpu.make_async_copy(gate_hbm, gate, sems.at[1])]
    for copy in copies:
        copy.start()
    index = lax.axis_index("seq")
    is_first = index % 2 == 0
    first = index * tok
    inner, per = gate.shape[1], heads // GROUPS
    columns = inner // GROUPS
    ends = ends_ref[...]
    position = lax.broadcasted_iota(jnp.int32, (tok, 128), 0) + first
    starts = start_of(ends, position)
    final = start_at(ends, first + tok - 1)
    column = lax.broadcasted_iota(jnp.int32, (tok, tok + 2 * RIM), 1)
    places = jnp.where(column < tok, column, jnp.where(column < tok + RIM, column - tok - RIM, tok))
    moves = shifts(starts, first, places, taps.shape[0])

    def rim_rows(lanes):
        if lanes.start < inner:
            second, at = divmod(lanes.start, inner // PAIR)
            return unpacked(rim, slice(at, at + BLOCK), second == 1)
        at = inner // PAIR + (lanes.start - inner) // PAIR
        halves = [unpacked(rim, slice(at, at + BLOCK // PAIR), k == 1) for k in range(PAIR)]
        return jnp.concatenate(halves, axis=1)

    def mixed(lanes):
        top = pick(is_first, rim_rows(lanes), other[tok - RIM :, lanes].astype(F32))
        extra = jnp.concatenate([top, jnp.zeros_like(top)], axis=0).astype(BF16)
        rows = jnp.concatenate([own[:, lanes], extra], axis=0)
        return convolve(moves, rows, taps[:, lanes], bias[lanes].reshape(1, lanes.stop - lanes.start)).astype(F32)

    step, sums = log_sums(raw[...], step_bias[...], rate_log[...])
    ending_decay = jnp.exp(sums[tok - 1 :])
    passed = jnp.where(final[:, :heads] < first, ending_decay, 0.0)
    rest = jnp.concatenate([ending_decay, passed, skip[...], jnp.zeros((5, heads), F32)], axis=0)
    whole = jnp.concatenate([jnp.exp(sums), jnp.exp(-sums) * step, rest], axis=0)
    chosen = selector(per, columns, width, 0)
    down, across = (lax.broadcasted_iota(jnp.int32, (tok, tok), k) for k in range(2))
    causal = (down >= across) & (across + first >= starts[:, :tok])
    here = position[:, :state] >= final[:, :state]
    entered = jnp.concatenate([starts] * (BLOCK // 128), axis=1) < first
    copies[0].wait()
    b_all, c_all = [], []
    for j in range(2 * GROUPS * state // BLOCK):
        pieces = mixed(slice(inner + j * BLOCK, inner + (j + 1) * BLOCK))
        for k in range(BLOCK // state):
            (b_all if len(b_all) < GROUPS else c_all).append(pieces[:, k * state : (k + 1) * state].astype(BF16))
    copies[1].wait()
    for g in range(GROUPS):
        wide = widen(whole[:, g * per : (g + 1) * per], chosen)
        b_rows, c_rows = b_all[g], c_all[g]
        c_out[g] = c_rows
        mask = jnp.where(causal, dot(c_rows, b_rows, ((1,), (1,))), 0.0)
        m_top, m_rest = split(mask, 2)
        lhs = jnp.concatenate([m_top.astype(F32), m_rest.astype(F32)], axis=1).astype(BF16)
        ending = jnp.where(here, b_rows.astype(F32), 0.0).astype(BF16)
        for j in range(columns // BLOCK):
            part = slice(j * BLOCK, (j + 1) * BLOCK)
            lanes = slice(g * columns + j * BLOCK, g * columns + (j + 1) * BLOCK)
            inward, outward = wide[:tok, part], wide[tok : 2 * tok, part]
            end_decay, gain = wide[2 * tok : 2 * tok + 1, part], wide[2 * tok + 2 : 2 * tok + 3, part]
            x = mixed(lanes)
            s_top, s_rest = split(x * outward, 2)
            within = dot(lhs, jnp.concatenate([s_top, s_top], axis=0)) + dot(m_top, s_rest)
            local = dot(ending, s_top, ((0,), (0,))) + dot(ending, s_rest, ((0,), (0,)))
            opened = silu(gate[:, lanes].astype(F32))
            a_out[:, lanes] = (inward * within + gain * x) * opened
            b_out[:, lanes] = jnp.where(entered, inward * opened, 0.0)
            s_out[:state, lanes] = (end_decay * local).astype(BF16)
        s_out[state:, g * columns : (g + 1) * columns] = two_rows(wide[2 * tok + 1 : 2 * tok + 2], (8, columns))


def place_of(far_core, far_row):
    index = lax.axis_index("seq")
    core, row = index % 2, (index // 2) % 2
    return PAIR * (1 - core if far_core else core) + (1 - row if far_row else row)


def finish_piece(width, group, arrived, a_ref, b_ref, c_ref, prior, gain, put):
    second = lax.axis_index("seq") % 2 == 1
    state_rows, columns = arrived.shape
    block = BLOCK
    down, across = (lax.broadcasted_iota(jnp.int32, (block, block), k) for k in range(2))
    low = across - lax.rem(across, width)
    means = jnp.where((down >= low) & (down < low + width), 1.0 / width, 0.0).astype(BF16)
    c_rows = c_ref[group]
    for j in range(columns // block):
        lanes = slice(j * block, (j + 1) * block)
        at = pl.ds(pl.multiple_of(group * columns + j * block, block), block)
        state = arrived[:, lanes].astype(F32)
        before = prior[:, at].astype(F32)
        stepped = (before[state_rows : state_rows + 1] + before[state_rows + 1 : state_rows + 2]) * state + before[:state_rows]
        state = pick(second, stepped, state).astype(BF16)
        gated = a_ref[:, at] + b_ref[:, at] * dot(c_rows, state)
        mean = dot((gated * gated).astype(BF16), means)
        put(lanes, (gated * lax.rsqrt(mean + EPSILON) * gain[:, at]).astype(BF16))


def finish_near_kernel(width, a, b, c, prior, gain, x0, x2, out, ready, sems):
    columns, copies = x0.shape[1], []
    for k, arrived in enumerate((x0, x2)):
        group = place_of(k == 1, False)

        def put(lanes, value, k=k):
            ready[k, :, lanes] = value

        finish_piece(width, group, arrived, a, b, c, prior, gain, put)
        target = out.at[:, pl.ds(pl.multiple_of(group * columns, columns), columns)]
        copies.append(pltpu.make_async_copy(ready.at[k], target, sems.at[k]))
        copies[-1].start()
    for copy in copies:
        copy.wait()


def finish_back_kernel(width, a, b, c, prior, gain, x1, out):
    def put(lanes, value):
        out[:, lanes] = value

    finish_piece(width, place_of(False, True), x1, a, b, c, prior, gain, put)


def finish_far_kernel(width, a, b, c, prior, gain, x3, piece, begun, out, ready, sems):
    columns = x3.shape[1]

    def target(group):
        return out.at[:, pl.ds(pl.multiple_of(group * columns, columns), columns)]

    early = pltpu.make_async_copy(piece, target(place_of(False, True)), sems.at[0])
    early.start()

    def put(lanes, value):
        ready[:, lanes] = value

    group = place_of(True, True)
    finish_piece(width, group, x3, a, b, c, prior, gain, put)
    copy = pltpu.make_async_copy(ready, target(group), sems.at[1])
    copy.start()
    early.wait()
    copy.wait()


def swap(block, pairs):
    return lax.ppermute(block, "seq", [*pairs, *((b, a) for a, b in pairs)])


def on_device(mixer_in, gate_in, step_raw, step_bias, rate_log, conv_weight, conv_bias, skip_gain, norm_gain, doc_lengths):
    tok, channels = mixer_in.shape
    heads, inner = rate_log.shape[0], gate_in.shape[1]
    width = inner // heads
    state = (channels - inner) // (2 * GROUPS)
    devices = lax.axis_size("seq")
    planes = devices // GROUPS
    columns = inner // GROUPS
    taps_n = conv_weight.shape[0]
    longest = devices * tok // 2
    reach = -(-(longest - 1) // (GROUPS * tok))
    row = lambda a: a.reshape(1, -1)
    step_bias, rate_log, skip_gain, norm_gain = map(row, (step_bias, rate_log, skip_gain, norm_gain))
    cores = [(i, i + 1) for i in range(0, devices, 2)]
    rows = [(i, i + 2) for i in range(0, devices, 4) for i in (i, i + 1)]
    chips = [(i, i + 1) for i in range(1, devices - 1, 2)]

    def hbm(block):
        return pltpu.with_memory_space_constraint(block, pltpu.HBM)

    other = swap(mixer_in, cores)
    other_raw = swap(step_raw, cores)
    own, rim, raw, step_bias, rate_log, taps, bias, ends = pl.pallas_call(
        functools.partial(load_kernel, (inner, PAIR * state)),
        out_shape=(
            jax.ShapeDtypeStruct((tok, channels), BF16), jax.ShapeDtypeStruct((RIM, channels // PAIR), BF16),
            jax.ShapeDtypeStruct((tok, heads), BF16), jax.ShapeDtypeStruct((1, heads), F32),
            jax.ShapeDtypeStruct((1, heads), F32), jax.ShapeDtypeStruct((taps_n, channels), F32),
            jax.ShapeDtypeStruct((channels,), F32), jax.ShapeDtypeStruct((doc_lengths.shape[0], 128), jnp.int32),
        ),
        in_specs=[HBM] * 7,
        out_specs=(VMEM,) * 8,
        scratch_shapes=[pltpu.SMEM(doc_lengths.shape, jnp.int32), pltpu.VMEM((RIM, channels), BF16), pltpu.SemaphoreType.DMA((9,))],
        compiler_params=pltpu.CompilerParams(vmem_limit_bytes=4 << 20),
        name="load",
    )(*map(hbm, (doc_lengths, mixer_in, step_raw, step_bias, rate_log, conv_weight, conv_bias)))
    rim = swap(rim, chips)
    other_rim = swap(rim, cores)

    def params(mib):
        return pltpu.CompilerParams(vmem_limit_bytes=mib << 20)

    packed = jax.ShapeDtypeStruct(((state + 2) * (columns // 128), 128), BF16)
    packed_wide = jax.ShapeDtypeStruct((state + 8, columns), F32)
    piece = jax.ShapeDtypeStruct((state, columns), BF16)
    dims = (heads, width, inner, tok)

    def states(keep, *operands):
        compact = () if keep else (jax.ShapeDtypeStruct((2 * tok + 16, heads), F32),)
        return pl.pallas_call(
            functools.partial(states_kernel, keep, dims, state),
            out_shape=(packed_wide if keep else packed, *compact),
            in_specs=[VMEM] * (3 + len(operands) + 2),
            out_specs=(VMEM,) * (1 + len(compact)),
            scratch_shapes=[pltpu.VMEM((2 * tok, columns), BF16)],
            compiler_params=params(8),
            name="states_kept" if keep else "states_sent",
        )(ends, own, other, *operands, taps, bias)

    sent, compact = states(False, raw, other_raw, step_bias, rate_log)
    got = swap(sent, rows)
    kept, = states(True, compact)
    corner = jax.ShapeDtypeStruct((RIM, columns + 128), BF16)
    rim_sent, rim_kept = pl.pallas_call(
        functools.partial(rim_kernel, dims),
        out_shape=(corner, corner),
        in_specs=[VMEM] * 8,
        out_specs=(VMEM, VMEM),
        compiler_params=params(4),
        name="rim_terms",
    )(ends, own, other, rim, other_rim, compact, taps, bias)
    rim_got = swap(rim_sent, rows)
    plane, far, base = pl.pallas_call(
        functools.partial(plane_kernel, state), out_shape=(packed, piece, packed_wide), in_specs=[VMEM] * 4, out_specs=(VMEM,) * 3,
        compiler_params=params(4), name="plane_total",
    )(kept, rim_kept, got, rim_got)
    parts = []
    for back in range(1, reach + 1):
        for parity in range(2):
            pairs = [
                (GROUPS * p + q, GROUPS * (p + back) + q)
                for p in range(planes - back) if p // back % 2 == parity
                for q in range(GROUPS)
            ]
            payload = far if back == reach else plane
            parts.append(swap(payload, pairs) if pairs else parts[-1])

    a, b, c, own_state = pl.pallas_call(
        functools.partial(local_kernel, (heads, width, state, tok)),
        out_shape=(
            jax.ShapeDtypeStruct((tok, inner), F32),
            jax.ShapeDtypeStruct((tok, inner), F32),
            jax.ShapeDtypeStruct((GROUPS, tok, state), BF16),
            jax.ShapeDtypeStruct((state + 8, inner), BF16),
        ),
        in_specs=[VMEM, HBM, VMEM, VMEM, HBM] + [VMEM] * 6,
        out_specs=(VMEM,) * 4,
        scratch_shapes=[pltpu.VMEM((tok, inner), BF16), pltpu.VMEM((tok, channels), BF16), pltpu.SemaphoreType.DMA((2,))],
        compiler_params=params(16),
        name="local_block",
    )(ends, hbm(mixer_in), other, rim, hbm(gate_in), raw, step_bias, rate_log, taps, bias, skip_gain)
    prior = swap(own_state, cores)

    x0, mine = pl.pallas_call(
        functools.partial(arrive_kernel, reach, state), out_shape=(piece, piece), in_specs=[VMEM] * (1 + 2 * reach),
        out_specs=(VMEM, VMEM), compiler_params=params(4), name="arrive",
    )(base, *parts)
    x1 = swap(mine, rows)
    x2 = swap(x0, cores)
    x3 = swap(x1, cores)

    common = (a, b, c, prior, norm_gain)
    whole_out = jax.ShapeDtypeStruct((tok, inner), BF16)
    ready = [pltpu.VMEM((2, tok, columns), BF16), pltpu.SemaphoreType.DMA((2,))]
    out = pl.pallas_call(
        functools.partial(finish_near_kernel, width), out_shape=whole_out, in_specs=[VMEM] * 7, out_specs=HBM,
        scratch_shapes=ready, compiler_params=params(8), name="finish_near",
    )(*common, x0, x2)
    back_piece = pl.pallas_call(
        functools.partial(finish_back_kernel, width), out_shape=jax.ShapeDtypeStruct((tok, columns), BF16),
        in_specs=[VMEM] * 6, out_specs=VMEM, compiler_params=params(8), name="finish_back",
    )(*common, x1)
    return pl.pallas_call(
        functools.partial(finish_far_kernel, width), out_shape=whole_out, in_specs=[VMEM] * 7 + [HBM], out_specs=HBM,
        scratch_shapes=[pltpu.VMEM((tok, columns), BF16), pltpu.SemaphoreType.DMA((2,))],
        input_output_aliases={7: 0}, compiler_params=params(8), name="finish_far",
    )(*common, x3, back_piece, out)


def solution(mesh):
    split_rows = P(("groups", "seq"), None)
    return jax.shard_map(
        on_device,
        mesh=mesh,
        in_specs=(split_rows, split_rows, split_rows, P(), P(), P(), P(), P(), P(), P("groups")),
        out_specs=split_rows,
        check_vma=False,
    )
```
